32 devices in a mesh: arrays: 2 (over y), tm: 8 (over z, x), chan: 2 (over core).
Axes of the slice: x: 2, y: 2, z: 4, core: 2. Of those that a mesh axis runs over, the one named last changes fastest.
Arguments:
- spectra: bfloat16 [128, 256, 2, 128], P(('arrays', 'tm'), 'chan'), parts along dimension 0, may hold values from -40 to 40
- offsets: int32 [128], P(('arrays', 'tm')), parts along dimension 0, may hold values from 0 to 63
- channel_group: int32 [512], P(('arrays', 'chan')), parts along dimension 0, may hold values from 0 to 7
Outputs:
- stack: float32 [128, 48, 128], P(('arrays', 'tm', 'chan')), parts along dimension 0
The draws below stay inside these ranges and needn't reach their ends.
There are 2 independent parts, one for each index of `arrays`. The reference program is written for one: setup_inputs(seed, part) draws one part's arguments, and reference() takes and returns one part's arrays. A program takes and returns all parts, laid end to end along the dimension named above; each array names one. Nothing has to cross between parts.
All inputs are finite; a program needn't handle non-finite values.
Results may differ from the reference program's by a relative error of at most 0.0075.
Values may be sent and summed in bfloat16 or wider, within the bound.
A program may use at most 64 MiB of HBM per device.

```python
import math
import jax
import jax.numpy as jnp
from jax import lax

F = 128
LAGS = 128
GROUPS = 8
BAND = 48
WINDOWS = 64
CHANNELS = 256


def draw_spectra(key, part):
    key_amplitude = jax.random.fold_in(key, 11)
    key_values = jax.random.fold_in(key, 12)
    amplitude = jnp.exp(jax.random.uniform(key_amplitude, (WINDOWS, CHANNELS, 1, 1), jnp.float32, math.log(0.1), math.log(10.0)))
    values = jnp.clip(jax.random.normal(key_values, (WINDOWS, CHANNELS, 2, F), jnp.float32), -4.0, 4.0)
    return (amplitude * values).astype(jnp.bfloat16)


def plant(result, key, low, high):
    longest = result.shape.index(max(result.shape))
    spots = []
    for shift in (0, 1):
        where = [jax.random.randint(jax.random.fold_in(key, axis), (), 0, length) for axis, length in enumerate(result.shape)]
        where[longest] = (where[longest] + shift) % result.shape[longest]
        spots.append(tuple(where))
    return result.at[spots[0]].set(low).at[spots[1]].set(high)


def setup_inputs(seed: int = 0, part: int = 0) -> dict:
    key_of = jax.random.split(jax.random.key(seed), 4)
    part_splits = jax.random.split(jax.random.fold_in(key_of[3], part), 4)
    return {
        "spectra": draw_spectra(jax.random.fold_in(jax.random.fold_in(key_of[3], part), 71), part),
        "offsets": plant(jax.random.randint(part_splits[1], (WINDOWS,), 0, LAGS // 2), jax.random.fold_in(part_splits[1], 1), 0, (LAGS // 2) - 1).astype(jnp.int32),
        "channel_group": plant(jax.random.randint(part_splits[2], (CHANNELS,), 0, GROUPS), jax.random.fold_in(part_splits[2], 1), 0, GROUPS - 1).astype(jnp.int32),
    }


epsilon = 1e-05

def lag_table(freq_bins, lag_count):
    frequency = jnp.arange(freq_bins, dtype=jnp.int32)[:, None]
    lag_shift = jnp.arange(lag_count, dtype=jnp.int32)[None, :] - lag_count // 2
    phase_turns = jnp.mod(frequency * lag_shift, 2 * freq_bins).astype(jnp.float32)
    phase_angle = jnp.pi * phase_turns / freq_bins
    normaliser = 1.0 / math.sqrt(freq_bins)
    lag_rows = jnp.concatenate([jnp.cos(phase_angle) * normaliser, -jnp.sin(phase_angle) * normaliser], axis=0)
    return lag_rows.astype(jnp.bfloat16)

def align_spectra(spectra, offsets, scales):
    freq_bins = spectra.shape[3]
    frequency = jnp.arange(freq_bins, dtype=jnp.int32)[None, :]
    phase_turns = jnp.mod(offsets[:, None] * frequency, 2 * freq_bins).astype(jnp.float32)
    phase_angle = jnp.pi * phase_turns / freq_bins
    cosine = jnp.cos(phase_angle)[:, None, :]
    sine_part = jnp.sin(phase_angle)[:, None, :]
    real_part = spectra[:, :, 0, :].astype(jnp.float32)
    imag_part = spectra[:, :, 1, :].astype(jnp.float32)
    weight = scales[:, :, None]
    out_real = weight * (real_part * cosine + imag_part * sine_part)
    out_imag = weight * (imag_part * cosine - real_part * sine_part)
    return jnp.stack([out_real, out_imag], axis=2).astype(jnp.bfloat16)

def window_terms(current, band_rows, lag_rows):
    left_real = current[None, :, 0, :].astype(jnp.float32)
    left_imag = current[None, :, 1, :].astype(jnp.float32)
    right_real = band_rows[:, :, 0, :].astype(jnp.float32)
    right_imag = band_rows[:, :, 1, :].astype(jnp.float32)
    prod_real = left_real * right_real + left_imag * right_imag
    prod_imag = left_imag * right_real - left_real * right_imag
    cross_spec = jnp.stack([prod_real, prod_imag], axis=2).astype(jnp.bfloat16)
    flattened = cross_spec.reshape(band_rows.shape[0] * band_rows.shape[1], 2 * band_rows.shape[3])
    lagged = jnp.dot(flattened.astype(jnp.float32), lag_rows.astype(jnp.float32), precision=lax.Precision.HIGHEST)
    lagged = lagged.reshape(band_rows.shape[0], band_rows.shape[1], lag_rows.shape[1])
    return lax.optimization_barrier(jnp.sum(lagged * lagged, axis=1))

def reference(spectra, offsets, channel_group):
    chan_power = lax.optimization_barrier(jnp.sum(jnp.square(spectra.astype(jnp.float32)), axis=(2, 3)))
    onehot = (channel_group[:, None] == jnp.arange(GROUPS, dtype=jnp.int32)[None, :]).astype(jnp.float32)
    group_total = jnp.dot(chan_power, onehot, precision=lax.Precision.HIGHEST)
    energy = group_total * (GROUPS / (F * CHANNELS))
    scales = jnp.dot(lax.rsqrt(energy + epsilon), onehot.T, precision=lax.Precision.HIGHEST)
    aligned = align_spectra(spectra, offsets, scales)
    padded = jnp.concatenate([jnp.zeros((BAND, CHANNELS, 2, F), jnp.bfloat16), aligned], axis=0)
    lag_rows = lag_table(F, LAGS)

    def one_window(window):
        current = lax.dynamic_index_in_dim(aligned, window, 0, keepdims=False)
        band_rows = lax.dynamic_slice_in_dim(padded, window, BAND, 0)
        return window_terms(current, band_rows, lag_rows)
    summed = lax.map(one_window, jnp.arange(WINDOWS, dtype=jnp.int32))
    return summed * (1.0 / CHANNELS)
```

```python
import functools
import math

import jax
import jax.numpy as jnp
from jax import lax
from jax.experimental import pallas as pl
from jax.experimental.pallas import tpu as pltpu
from jax.sharding import PartitionSpec as P

LAGS = 128
GROUPS = 8
SPAN = 6


epsilon = 1e-05


def shifted(value, axis, steps):
    count = lax.axis_size(axis)
    initial, last = (max(0, -steps), min(count, count - steps))
    return lax.ppermute(value, axis, [(source, source + steps) for source in range(initial, last)])


def lag_table(freq_bins, lag_count):
    frequency = jnp.arange(freq_bins, dtype=jnp.int32)[:, None]
    lag_shift = jnp.arange(lag_count, dtype=jnp.int32)[None, :] - lag_count // 2
    phase_turns = jnp.mod(frequency * lag_shift, 2 * freq_bins).astype(jnp.float32)
    phase_angle = jnp.pi * phase_turns / freq_bins
    normaliser = 1.0 / math.sqrt(freq_bins)
    lag_rows = jnp.concatenate(
        [jnp.cos(phase_angle) * normaliser, -jnp.sin(phase_angle) * normaliser], axis=0
    )
    return lag_rows.astype(jnp.bfloat16)


def align_spectra(spectra, offsets, scales):
    freq_bins = spectra.shape[3]
    frequency = jnp.arange(freq_bins, dtype=jnp.int32)[None, :]
    phase_turns = jnp.mod(offsets[:, None] * frequency, 2 * freq_bins).astype(jnp.float32)
    phase_angle = jnp.pi * phase_turns / freq_bins
    cosine = jnp.cos(phase_angle)[:, None, :]
    sine_part = jnp.sin(phase_angle)[:, None, :]
    real_part = spectra[:, :, 0, :].astype(jnp.float32)
    imag_part = spectra[:, :, 1, :].astype(jnp.float32)
    weight = scales[:, :, None]
    out_real = weight * (real_part * cosine + imag_part * sine_part)
    out_imag = weight * (imag_part * cosine - real_part * sine_part)
    return jnp.stack([out_real, out_imag], axis=2).astype(jnp.bfloat16)


def window_terms(current, band_rows, lag_rows):
    left_real = current[None, :, 0, :].astype(jnp.float32)
    left_imag = current[None, :, 1, :].astype(jnp.float32)
    right_real = band_rows[:, :, 0, :].astype(jnp.float32)
    right_imag = band_rows[:, :, 1, :].astype(jnp.float32)
    prod_real = left_real * right_real + left_imag * right_imag
    prod_imag = left_imag * right_real - left_real * right_imag
    cross_spec = jnp.stack([prod_real, prod_imag], axis=2).astype(jnp.bfloat16)
    flattened = cross_spec.reshape(band_rows.shape[0] * band_rows.shape[1], 2 * band_rows.shape[3])
    lagged = jnp.dot(flattened, lag_rows, preferred_element_type=jnp.float32)
    lagged = lagged.reshape(band_rows.shape[0], band_rows.shape[1], lag_rows.shape[1])
    return jnp.sum(lagged * lagged, axis=1)


def ring_shards(spectra, offsets, channel_group):
    windows = spectra.shape[0]
    local_chans = spectra.shape[1]
    freq_bins = spectra.shape[3]
    chan_count = lax.axis_size("chan")
    channels = local_chans * chan_count
    onehot = (channel_group[:, None] == jnp.arange(GROUPS, dtype=jnp.int32)[None, :]).astype(
        jnp.float32
    )
    chan_power = jnp.sum(jnp.square(spectra.astype(jnp.float32)), axis=(2, 3))
    partial_value = jnp.dot(chan_power, onehot, precision=lax.Precision.HIGHEST)
    group_total = lax.psum(partial_value, "chan")
    energy = group_total * (GROUPS / (freq_bins * channels))
    scales = jnp.dot(lax.rsqrt(energy + epsilon), onehot.T, precision=lax.Precision.HIGHEST)
    aligned = align_spectra(spectra, offsets, scales)
    earlier = []
    carried = aligned
    for distance in range(SPAN):
        carried = shifted(carried, "tm", 1)
        earlier.append(carried)
    buffer = jnp.concatenate(earlier[::-1] + [aligned], axis=0)
    lag_rows = lag_table(freq_bins, LAGS)
    band_len = SPAN * windows

    def one_window(window):
        current = lax.dynamic_index_in_dim(aligned, window, 0, keepdims=False)
        band_rows = lax.dynamic_slice_in_dim(buffer, window, band_len, 0)
        return window_terms(current, band_rows, lag_rows) * (1.0 / channels)

    return lax.psum_scatter(
        lax.map(
            one_window, jnp.arange(lax.axis_size("chan") * (windows // chan_count), dtype=jnp.int32)
        ).astype(jnp.bfloat16),
        "chan",
        scatter_dimension=0,
        tiled=True,
    ).astype(jnp.float32)


HIGHEST = lax.Precision.HIGHEST
PAIR = 2
COLUMNS = 2
PARTS = 4


def phase_of(turns, freq_bins):
    period = 2.0 * freq_bins
    return (jnp.pi / freq_bins) * (turns - period * jnp.floor(turns / period))


def kernel(
    n, chans, windows, freq_bins, cores,
    x_ref, off_ref, group_ref, out_ref,
    local, wide, sums, tile, tile_in, al, right, left, table, acc, total, sum_out, sum_in,
    local_sem, own_sem, e_send, e_recv, x_send, x_recv, f_send, f_recv, s_send, s_recv, ready,
):
    me = lax.axis_index("tm")
    core = lax.axis_index("chan")
    levels = n // COLUMNS
    level, column = me // COLUMNS, lax.rem(me, COLUMNS)
    half = level // 2
    inner = jnp.logical_or(level == 1, level == levels - 2)
    blocks = n // 2
    mine = windows // cores
    lanes = freq_bins
    bf16 = jnp.bfloat16
    groups = chans // windows
    chunk = groups // PARTS
    pairs = windows // PAIR
    mesh_id = pl.DeviceIdType.MESH

    load = pltpu.make_async_copy(x_ref, local, local_sem)
    load.start()

    barrier = pltpu.get_barrier_semaphore()
    beside = COLUMNS * level + 1 - column
    above, below = level + 1 < levels, level > 0

    def greet(sem):
        pl.semaphore_signal(sem, inc=1, device_id={"tm": beside}, device_id_type=mesh_id)

        @pl.when(above)
        def _():
            pl.semaphore_signal(sem, inc=1, device_id={"tm": me + COLUMNS}, device_id_type=mesh_id)

        @pl.when(below)
        def _():
            pl.semaphore_signal(sem, inc=1, device_id={"tm": me - COLUMNS}, device_id_type=mesh_id)

    near = 1 + jnp.where(above, 1, 0) + jnp.where(below, 1, 0)
    pl.semaphore_signal(barrier, inc=1, device_id={"chan": 1 - core}, device_id_type=mesh_id)
    greet(barrier)

    frequency = lax.broadcasted_iota(jnp.int32, (freq_bins, LAGS), 0)
    shift = lax.broadcasted_iota(jnp.int32, (freq_bins, LAGS), 1) - LAGS // 2
    group_id = lax.broadcasted_iota(jnp.int32, (lanes, chans), 0)
    onehot = (group_id == group_ref[...]).astype(jnp.float32)
    few = onehot[:GROUPS].astype(bf16)
    both = jnp.concatenate([few, few], axis=1)
    lane = lax.broadcasted_iota(jnp.int32, (windows, lanes), 1)
    row = lax.broadcasted_iota(jnp.int32, (windows, lanes), 0)

    load.wait()
    for w in range(windows):
        wide[pl.ds(w * 2 * chans, 2 * chans), :] = local[w].astype(jnp.float32)
    for w in range(windows):
        real = wide[pl.ds(w * 2 * chans, chans, stride=2), :]
        imag = wide[pl.ds(w * 2 * chans + 1, chans, stride=2), :]
        power = real * real + imag * imag
        high = power.astype(bf16)
        low = (power - high.astype(jnp.float32)).astype(bf16)
        sums[pl.ds(w * GROUPS, GROUPS), :] = jnp.dot(
            both, jnp.concatenate([high, low], axis=0), preferred_element_type=jnp.float32
        )
    totals = jnp.zeros((windows, lanes), jnp.float32)
    for g in range(GROUPS):
        held = jnp.sum(sums[pl.ds(g, windows, stride=GROUPS), :], axis=1, keepdims=True)
        totals = jnp.where(lane == g, held, totals)
    tile[...] = totals
    e_copy = pltpu.make_async_remote_copy(
        src_ref=tile, dst_ref=tile_in, send_sem=e_send, recv_sem=e_recv,
        device_id={"chan": 1 - core}, device_id_type=mesh_id,
    )
    pl.semaphore_wait(barrier, near + 1)
    e_copy.start()
    greet(ready.at[0])

    angle = phase_of((frequency * shift).astype(jnp.float32), freq_bins)
    normaliser = 1.0 / math.sqrt(freq_bins)
    table[pl.ds(0, freq_bins), :] = (jnp.cos(angle) * normaliser).astype(bf16)
    table[pl.ds(freq_bins, freq_bins), :] = (-jnp.sin(angle) * normaliser).astype(bf16)
    starts = jnp.zeros((windows, lanes), jnp.float32)
    for w in range(windows):
        starts = jnp.where(row == w, off_ref[w].astype(jnp.float32), starts)
    theta = phase_of(lane.astype(jnp.float32) * starts, freq_bins)
    cosine = jnp.cos(theta)
    sine = jnp.sin(theta)
    acc[...] = jnp.zeros_like(acc)
    total[:, pl.ds(0, SPAN * windows), :] = jnp.zeros((mine, SPAN * windows, LAGS), jnp.float32)

    pl.semaphore_wait(ready.at[0], near)
    greet(ready.at[1])
    e_copy.wait_recv()
    energy = (totals + tile_in[...]) * (GROUPS / (freq_bins * chans * cores))
    scales = jnp.dot(lax.rsqrt(energy + epsilon), onehot, precision=HIGHEST, preferred_element_type=jnp.float32)

    def aligned(c):
        real = wide[pl.ds(2 * c, windows, stride=2 * chans), :]
        imag = wide[pl.ds(2 * c + 1, windows, stride=2 * chans), :]
        weight = scales[:, c : c + 1]
        return weight * (real * cosine + imag * sine), weight * (imag * cosine - real * sine)

    for g in range(groups):
        for p in range(pairs):
            one, two = (aligned((g * pairs + p) * PAIR + i) for i in range(PAIR))
            for r in range(2):
                al[g, 2 * p + r] = jnp.concatenate([one[r], two[r]], axis=0).astype(bf16)
    pl.semaphore_wait(ready.at[1], near)

    def routes():
        for own in (1, 0):
            for flip in range(COLUMNS):
                place = COLUMNS * jnp.where(own == 1, half, 1 - half) + (column if flip == 0 else 1 - column)
                yield COLUMNS + place, chunk * place, 0, 2 * (1 - own) + flip
        for part in range(2):
            for flip in range(COLUMNS):
                place = column if flip == 0 else 1 - column
                yield (n - COLUMNS) * half + place, chunk * (2 * place + part), part, 4 + 2 * part + flip

    def slot(part, of):
        return (part * cores + of) * chunk

    def x_copy(there, first, part, index, source):
        return pltpu.make_async_remote_copy(
            src_ref=al.at[pl.ds(first, chunk)],
            dst_ref=right.at[source, pl.ds(slot(part, core), chunk)],
            send_sem=x_send.at[index],
            recv_sem=x_recv.at[source, part],
            device_id={"tm": there},
            device_id_type=mesh_id,
        )

    def own_copy(first, part):
        return pltpu.make_async_copy(
            al.at[pl.ds(first, chunk)], right.at[me, pl.ds(slot(part, core), chunk)], own_sem.at[part]
        )

    def f_copy(t, part):
        return pltpu.make_async_remote_copy(
            src_ref=right.at[t, pl.ds(slot(part, core), chunk)],
            dst_ref=right.at[t, pl.ds(slot(part, core), chunk)],
            send_sem=f_send.at[t, part],
            recv_sem=f_recv.at[t, part],
            device_id={"chan": 1 - core},
            device_id_type=mesh_id,
        )

    for there, first, part, index in routes():
        @pl.when(there == me)
        def _():
            own_copy(first, part).start()

        @pl.when(there != me)
        def _():
            x_copy(there, first, part, index, me).start()

    bit = lax.rem(level, 2)

    def block(base, flip, k):
        return base + COLUMNS * lax.rem(bit + flip + k // 2, 2) + lax.rem(column + lax.rem(k, 2), 2)

    here, away = blocks * half, blocks * (1 - half)

    def job(upper, lower, first):
        up, low = lax.rem(upper, blocks), lax.rem(lower, blocks)
        for j in range(mine):
            rows = []
            at = core * mine + j
            for g in range(chunk):
                for p in range(pairs):
                    right_real = right[lower, first + g, 2 * p]
                    right_imag = right[lower, first + g, 2 * p + 1]
                    picked = [
                        jnp.concatenate(
                            [left[upper, first + g, 2 * p + r, pl.ds(i * windows + at, windows, stride=0), :] for i in range(PAIR)],
                            axis=0,
                        ).astype(bf16)
                        for r in range(2)
                    ]
                    left_real, left_imag = picked
                    rows.append(
                        jnp.concatenate(
                            [
                                left_real * right_real + left_imag * right_imag,
                                left_imag * right_real - left_real * right_imag,
                            ],
                            axis=1,
                        )
                    )
            lagged = jnp.dot(jnp.concatenate(rows, axis=0), table[...], preferred_element_type=jnp.float32)
            lagged = lagged.reshape(chunk * pairs * PAIR, windows, LAGS)
            acc[up, j, pl.ds(low * windows, windows), :] += jnp.sum(lagged * lagged, axis=0)

    holder = jnp.where(inner, me - COLUMNS, 2 * COLUMNS + column)
    target = blocks * jnp.where(inner, 1, half)

    def s_copy(local_t, source):
        return pltpu.make_async_remote_copy(
            src_ref=sum_out.at[local_t],
            dst_ref=sum_in.at[source],
            send_sem=s_send.at[local_t],
            recv_sem=s_recv.at[source],
            device_id={"tm": target + local_t},
            device_id_type=mesh_id,
        )

    def hand_over(local_t):
        @pl.when(target + local_t == me)
        def _():
            sum_in[holder] = acc[local_t].astype(bf16)

        @pl.when(target + local_t != me)
        def _():
            sum_out[local_t] = acc[local_t].astype(bf16)
            s_copy(local_t, holder).start()

    early = jnp.logical_and(inner, half == 0)

    def step(q, carry):
        part = jnp.where(inner, 0, q // blocks)
        i = lax.rem(q, blocks)
        far = jnp.logical_and(inner, q >= blocks)
        t = jnp.where(far, block(away, 1, i), block(here, 0, i))
        count = jnp.where(inner, jnp.where(far, blocks, 0), i + 1)

        @pl.when(t == me)
        def _():
            own_copy(0, part).wait()

        @pl.when(t != me)
        def _():
            x_copy(me, 0, part, 0, t).wait_recv()

        f_copy(t, part).start()

        def one_side(c, held):
            first = slot(part, lax.rem(core + c, cores))

            @pl.when(c > 0)
            def _():
                f_copy(t, part).wait_recv()

            for g in range(chunk):
                for r in range(2 * pairs):
                    left[t, first + g, r] = right[t, first + g, r].astype(jnp.float32)

            def one_job(k, inside):
                other = block(here, 0, k)
                upper, lower = jnp.maximum(t, other), jnp.minimum(t, other)

                @pl.when(upper - lower <= SPAN)
                def _():
                    job(upper, lower, first)

                return inside

            lax.fori_loop(0, count, one_job, 0)
            return held

        lax.fori_loop(0, cores, one_side, 0)

        @pl.when(jnp.logical_and(early, far))
        def _():
            hand_over(lax.rem(t, blocks))

        return carry

    lax.fori_loop(0, n, step, 0)

    @pl.when(jnp.logical_not(early))
    def _():
        for local_t in range(blocks):
            hand_over(local_t)

    def collect(first, count):
        result = None
        for source in range(first, first + count):
            @pl.when(source != holder_here)
            def _():
                s_copy(0, source).wait_recv()

            value = sum_in[source].astype(jnp.float32)
            result = value if result is None else result + value
        return result

    keeps = jnp.logical_and(me >= target, me < target + blocks)
    holder_here = jnp.where(keeps, holder, -1)
    base = SPAN * windows
    rows = blocks * windows
    intra = collect(2 * COLUMNS, COLUMNS)

    @pl.when(half == 0)
    def _():
        total[:, pl.ds(base, rows), :] = intra

    @pl.when(half == 1)
    def _():
        total[:, pl.ds(base + rows, rows), :] = intra
        total[:, pl.ds(base, rows), :] = collect(0, 2 * COLUMNS)

    for j in range(mine):
        out_ref[j] = total[j, pl.ds(me * windows + core * mine + j, base), :] * (1.0 / (chans * cores))

    for there, first, part, index in routes():
        @pl.when(there != me)
        def _():
            x_copy(there, first, part, index, me).wait_send()

    def sent(q, carry):
        part = jnp.where(inner, 0, q // blocks)
        i = lax.rem(q, blocks)
        far = jnp.logical_and(inner, q >= blocks)
        t = jnp.where(far, block(away, 1, i), block(here, 0, i))
        f_copy(t, part).wait_send()
        return carry

    lax.fori_loop(0, n, sent, 0)
    for local_t in range(blocks):
        @pl.when(target + local_t != me)
        def _():
            s_copy(local_t, holder).wait_send()
    e_copy.wait_send()


def spread_shards(spectra, offsets, channel_group):
    windows, chans, _, freq_bins = spectra.shape
    n = lax.axis_size("tm")
    cores = lax.axis_size("chan")
    blocks = n // 2
    groups = chans // windows
    band = SPAN * windows
    mine = windows // cores
    dma = pltpu.SemaphoreType.DMA
    tiles = (2 * (windows // PAIR), PAIR * windows, freq_bins)
    return pl.pallas_call(
        functools.partial(kernel, n, chans, windows, freq_bins, cores),
        out_shape=pltpu.VMEM((mine, band, LAGS), jnp.float32),
        in_specs=[
            pl.BlockSpec(memory_space=pl.ANY),
            pl.BlockSpec(memory_space=pltpu.SMEM),
            pl.BlockSpec(memory_space=pltpu.VMEM),
        ],
        out_specs=pl.BlockSpec(memory_space=pltpu.VMEM),
        scratch_shapes=[
            pltpu.VMEM((windows, 2 * chans, freq_bins), jnp.bfloat16),
            pltpu.VMEM((windows * 2 * chans, freq_bins), jnp.float32),
            pltpu.VMEM((windows * GROUPS, freq_bins), jnp.float32),
            pltpu.VMEM((windows, freq_bins), jnp.float32),
            pltpu.VMEM((windows, freq_bins), jnp.float32),
            pltpu.VMEM((groups,) + tiles, jnp.bfloat16),
            pltpu.VMEM((n, groups) + tiles, jnp.bfloat16),
            pltpu.VMEM((n, groups) + tiles, jnp.float32),
            pltpu.VMEM((2 * freq_bins, LAGS), jnp.bfloat16),
            pltpu.VMEM((blocks, mine, blocks * windows, LAGS), jnp.float32),
            pltpu.VMEM((mine, band + n * windows, LAGS), jnp.float32),
            pltpu.VMEM((blocks, mine, blocks * windows, LAGS), jnp.bfloat16),
            pltpu.VMEM((3 * COLUMNS, mine, blocks * windows, LAGS), jnp.bfloat16),
            dma, dma((2,)), dma, dma, dma((n,)), dma((n, 2)), dma((n, 2)), dma((n, 2)),
            dma((blocks,)), dma((3 * COLUMNS,)), pltpu.SemaphoreType.REGULAR((2,)),
        ],
        compiler_params=pltpu.CompilerParams(
            collective_id=0, has_side_effects=True, vmem_limit_bytes=56 * 1024 * 1024
        ),
    )(spectra.reshape(windows, 2 * chans, freq_bins), offsets, channel_group.reshape(1, chans))


def shards(spectra, offsets, channel_group):
    windows, chans, _, freq_bins = spectra.shape
    n = lax.axis_size("tm")
    fits = (
        chans == freq_bins == LAGS == 128
        and windows == 8
        and lax.axis_size("chan") == 2
        and n == 8
    )
    return (spread_shards if fits else ring_shards)(spectra, offsets, channel_group)


def solution(mesh):
    placed = (P(("arrays", "tm"), "chan", None, None), P(("arrays", "tm")), P(("arrays", "chan")))
    return jax.shard_map(
        shards,
        mesh=mesh,
        in_specs=placed,
        out_specs=P(("arrays", "tm", "chan"), None, None),
        check_vma=False,
    )
```

```python
import functools
import math

import jax
import jax.numpy as jnp
from jax import lax
from jax.experimental import pallas as pl
from jax.experimental.pallas import tpu as pltpu
from jax.sharding import PartitionSpec as P

LAGS = 128
GROUPS = 8
SPAN = 6


epsilon = 1e-05


def shifted(value, axis, steps):
    count = lax.axis_size(axis)
    initial, last = (max(0, -steps), min(count, count - steps))
    return lax.ppermute(value, axis, [(source, source + steps) for source in range(initial, last)])


def lag_table(freq_bins, lag_count):
    frequency = jnp.arange(freq_bins, dtype=jnp.int32)[:, None]
    lag_shift = jnp.arange(lag_count, dtype=jnp.int32)[None, :] - lag_count // 2
    phase_turns = jnp.mod(frequency * lag_shift, 2 * freq_bins).astype(jnp.float32)
    phase_angle = jnp.pi * phase_turns / freq_bins
    normaliser = 1.0 / math.sqrt(freq_bins)
    lag_rows = jnp.concatenate(
        [jnp.cos(phase_angle) * normaliser, -jnp.sin(phase_angle) * normaliser], axis=0
    )
    return lag_rows.astype(jnp.bfloat16)


def align_spectra(spectra, offsets, scales):
    freq_bins = spectra.shape[3]
    frequency = jnp.arange(freq_bins, dtype=jnp.int32)[None, :]
    phase_turns = jnp.mod(offsets[:, None] * frequency, 2 * freq_bins).astype(jnp.float32)
    phase_angle = jnp.pi * phase_turns / freq_bins
    cosine = jnp.cos(phase_angle)[:, None, :]
    sine_part = jnp.sin(phase_angle)[:, None, :]
    real_part = spectra[:, :, 0, :].astype(jnp.float32)
    imag_part = spectra[:, :, 1, :].astype(jnp.float32)
    weight = scales[:, :, None]
    out_real = weight * (real_part * cosine + imag_part * sine_part)
    out_imag = weight * (imag_part * cosine - real_part * sine_part)
    return jnp.stack([out_real, out_imag], axis=2).astype(jnp.bfloat16)


def window_terms(current, band_rows, lag_rows):
    left_real = current[None, :, 0, :].astype(jnp.float32)
    left_imag = current[None, :, 1, :].astype(jnp.float32)
    right_real = band_rows[:, :, 0, :].astype(jnp.float32)
    right_imag = band_rows[:, :, 1, :].astype(jnp.float32)
    prod_real = left_real * right_real + left_imag * right_imag
    prod_imag = left_imag * right_real - left_real * right_imag
    cross_spec = jnp.stack([prod_real, prod_imag], axis=2).astype(jnp.bfloat16)
    flattened = cross_spec.reshape(band_rows.shape[0] * band_rows.shape[1], 2 * band_rows.shape[3])
    lagged = jnp.dot(flattened, lag_rows, preferred_element_type=jnp.float32)
    lagged = lagged.reshape(band_rows.shape[0], band_rows.shape[1], lag_rows.shape[1])
    return jnp.sum(lagged * lagged, axis=1)


def ring_shards(spectra, offsets, channel_group):
    windows = spectra.shape[0]
    local_chans = spectra.shape[1]
    freq_bins = spectra.shape[3]
    chan_count = lax.axis_size("chan")
    channels = local_chans * chan_count
    onehot = (channel_group[:, None] == jnp.arange(GROUPS, dtype=jnp.int32)[None, :]).astype(
        jnp.float32
    )
    chan_power = jnp.sum(jnp.square(spectra.astype(jnp.float32)), axis=(2, 3))
    partial_value = jnp.dot(chan_power, onehot, precision=lax.Precision.HIGHEST)
    group_total = lax.psum(partial_value, "chan")
    energy = group_total * (GROUPS / (freq_bins * channels))
    scales = jnp.dot(lax.rsqrt(energy + epsilon), onehot.T, precision=lax.Precision.HIGHEST)
    aligned = align_spectra(spectra, offsets, scales)
    earlier = []
    carried = aligned
    for distance in range(SPAN):
        carried = shifted(carried, "tm", 1)
        earlier.append(carried)
    buffer = jnp.concatenate(earlier[::-1] + [aligned], axis=0)
    lag_rows = lag_table(freq_bins, LAGS)
    band_len = SPAN * windows

    def one_window(window):
        current = lax.dynamic_index_in_dim(aligned, window, 0, keepdims=False)
        band_rows = lax.dynamic_slice_in_dim(buffer, window, band_len, 0)
        return window_terms(current, band_rows, lag_rows) * (1.0 / channels)

    return lax.psum_scatter(
        lax.map(
            one_window, jnp.arange(lax.axis_size("chan") * (windows // chan_count), dtype=jnp.int32)
        ).astype(jnp.bfloat16),
        "chan",
        scatter_dimension=0,
        tiled=True,
    ).astype(jnp.float32)


HIGHEST = lax.Precision.HIGHEST
ROWS = 16
COLUMNS = 2
PARTS = 4
FAR = 2


def phase_of(turns, freq_bins):
    period = 2.0 * freq_bins
    return (jnp.pi / freq_bins) * (turns - period * jnp.floor(turns / period))


def kernel(
    n, chans, windows, freq_bins, cores,
    x_ref, off_ref, group_ref, out_ref,
    local, wide, sums, tile, tile_in, al, right, left, table, acc, total, sum_out, sum_in,
    local_sem, own_sem, e_send, e_recv, x_send, x_recv, s_send, s_recv, ready,
):
    me = lax.axis_index("tm")
    core = lax.axis_index("chan")
    levels = n // COLUMNS
    level, column = me // COLUMNS, lax.rem(me, COLUMNS)
    half = level // 2
    inner = jnp.logical_or(level == 1, level == levels - 2)
    blocks = n // 2
    mine = windows // cores
    lanes = freq_bins
    bf16 = jnp.bfloat16
    share = chans // PARTS
    tiles = share // ROWS
    mesh_id = pl.DeviceIdType.MESH

    loads = [pltpu.make_async_copy(x_ref.at[w], local.at[w], local_sem.at[w]) for w in range(windows)]
    for load in loads:
        load.start()

    barrier = pltpu.get_barrier_semaphore()
    beside = COLUMNS * level + 1 - column
    above, below = level + 1 < levels, level > 0

    def greet(sem):
        pl.semaphore_signal(sem, inc=1, device_id={"tm": beside}, device_id_type=mesh_id)

        @pl.when(above)
        def _():
            pl.semaphore_signal(sem, inc=1, device_id={"tm": me + COLUMNS}, device_id_type=mesh_id)

        @pl.when(below)
        def _():
            pl.semaphore_signal(sem, inc=1, device_id={"tm": me - COLUMNS}, device_id_type=mesh_id)

    near = 1 + jnp.where(above, 1, 0) + jnp.where(below, 1, 0)
    pl.semaphore_signal(barrier, inc=1, device_id={"chan": 1 - core}, device_id_type=mesh_id)
    greet(barrier)

    frequency = lax.broadcasted_iota(jnp.int32, (freq_bins, LAGS), 0)
    shift = lax.broadcasted_iota(jnp.int32, (freq_bins, LAGS), 1) - LAGS // 2
    group_id = lax.broadcasted_iota(jnp.int32, (GROUPS, chans), 0)
    onehot = (group_id == group_ref[...]).astype(jnp.float32)
    few = onehot.astype(bf16)
    both = jnp.concatenate([few, few], axis=1)
    member = jnp.concatenate([few, few, few, few], axis=0)
    lane = lax.broadcasted_iota(jnp.int32, (windows, lanes), 1)
    row = lax.broadcasted_iota(jnp.int32, (windows, lanes), 0)

    for w in range(windows):
        loads[w].wait()
        if w == windows - 1:
            pl.semaphore_wait(barrier, near + 1)
            greet(ready.at[0])
        wide[pl.ds(w * 2 * chans, 2 * chans), :] = local[w].astype(jnp.float32)
        real = wide[pl.ds(w * 2 * chans, chans, stride=2), :]
        imag = wide[pl.ds(w * 2 * chans + 1, chans, stride=2), :]
        power = real * real + imag * imag
        high = power.astype(bf16)
        low = (power - high.astype(jnp.float32)).astype(bf16)
        sums[pl.ds(w * GROUPS, GROUPS), :] = jnp.dot(
            both, jnp.concatenate([high, low], axis=0), preferred_element_type=jnp.float32
        )
    totals = jnp.broadcast_to(jnp.sum(sums[...], axis=1, keepdims=True), sums.shape)
    tile[...] = totals
    e_copy = pltpu.make_async_remote_copy(
        src_ref=tile, dst_ref=tile_in, send_sem=e_send, recv_sem=e_recv,
        device_id={"chan": 1 - core}, device_id_type=mesh_id,
    )
    e_copy.start()

    angle = phase_of((frequency * shift).astype(jnp.float32), freq_bins)
    normaliser = 1.0 / math.sqrt(freq_bins)
    table[pl.ds(0, freq_bins), :] = (jnp.cos(angle) * normaliser).astype(bf16)
    table[pl.ds(freq_bins, freq_bins), :] = (-jnp.sin(angle) * normaliser).astype(bf16)
    starts = jnp.zeros((windows, lanes), jnp.float32)
    for w in range(windows):
        starts = jnp.where(row == w, off_ref[w].astype(jnp.float32), starts)
    theta = phase_of(lane.astype(jnp.float32) * starts, freq_bins)
    cosine = jnp.cos(theta)
    sine = jnp.sin(theta)
    acc[...] = jnp.zeros_like(acc)
    total[:, pl.ds(0, SPAN * windows), :] = jnp.zeros((mine, SPAN * windows, LAGS), jnp.float32)

    pl.semaphore_wait(ready.at[0], near)
    greet(ready.at[1])
    e_copy.wait_recv()
    energy = (totals + tile_in[...]) * (GROUPS / (freq_bins * chans * cores))
    scales = lax.rsqrt(energy + epsilon)

    for w in range(windows):
        factor = scales[w * GROUPS : (w + 1) * GROUPS]
        turn = jnp.concatenate([factor * cosine[w : w + 1], factor * sine[w : w + 1]], axis=1)
        top = turn.astype(bf16)
        rest = turn - top.astype(jnp.float32)
        middle = rest.astype(bf16)
        bottom = (rest - middle.astype(jnp.float32)).astype(bf16)
        pieces = jnp.concatenate([top, middle, bottom, jnp.zeros_like(top)], axis=0)
        factors = lax.dot_general(
            member, pieces, (((0,), (0,)), ((), ())), preferred_element_type=jnp.float32
        )
        real = wide[pl.ds(w * 2 * chans, chans, stride=2), :]
        imag = wide[pl.ds(w * 2 * chans + 1, chans, stride=2), :]
        turn_cos, turn_sin = factors[:, :lanes], factors[:, lanes:]
        out = (real * turn_cos + imag * turn_sin, imag * turn_cos - real * turn_sin)
        for r in range(2):
            al[:, w, :, r] = out[r].astype(bf16).reshape(PARTS, tiles, ROWS, freq_bins)

    def routes():
        def inside(own, flip):
            place = COLUMNS * (half if own else 1 - half) + lax.rem(column + core + flip, 2)
            return COLUMNS + place, place, 0, 2 * (1 - own) + flip

        yield inside(1, 0)
        yield inside(0, 0)
        yield inside(0, 1)
        yield inside(1, 1)
        for part in range(2):
            for flip in range(COLUMNS):
                place = lax.rem(column + core + flip, 2)
                yield (n - COLUMNS) * half + place, 2 * place + part, part, 4 + 2 * part + flip

    def x_copy(there, first, part, index, source):
        return pltpu.make_async_remote_copy(
            src_ref=al.at[first],
            dst_ref=right.at[source, part],
            send_sem=x_send.at[index],
            recv_sem=x_recv.at[source, part],
            device_id={"tm": there},
            device_id_type=mesh_id,
        )

    def own_copy(first, part):
        return pltpu.make_async_copy(al.at[first], right.at[me, part], own_sem.at[part])

    for there, first, part, index in routes():
        if index == FAR:
            @pl.when(jnp.logical_not(inner))
            def _():
                pl.semaphore_wait(ready.at[1], near)

        @pl.when(there == me)
        def _():
            own_copy(first, part).start()

        @pl.when(there != me)
        def _():
            x_copy(there, first, part, index, me).start()

    @pl.when(inner)
    def _():
        pl.semaphore_wait(ready.at[1], near)

    greet(ready.at[2])

    bit = lax.rem(level, 2)

    def block(base, flip, k):
        turned = core * jnp.maximum(flip, k // 2)
        return base + COLUMNS * lax.rem(bit + flip + k // 2, 2) + lax.rem(column + turned + lax.rem(k, 2), 2)

    here, away = blocks * half, blocks * (1 - half)

    def job(sets, part):
        for w in range(windows):
            rows = []
            for upper, lower in sets:
                for i in range(tiles):
                    left_real = left[upper, part, w, i, 0].astype(bf16)
                    left_imag = left[upper, part, w, i, 1].astype(bf16)
                    for v in range(windows):
                        right_real = right[lower, part, v, i, 0]
                        right_imag = right[lower, part, v, i, 1]
                        rows.append(
                            jnp.concatenate(
                                [
                                    left_real * right_real + left_imag * right_imag,
                                    left_imag * right_real - left_real * right_imag,
                                ],
                                axis=1,
                            )
                        )
            lagged = jnp.dot(jnp.concatenate(rows, axis=0), table[...], preferred_element_type=jnp.float32)
            lagged = lagged.reshape(len(sets), tiles, windows, ROWS // 8, 8, LAGS)
            squares = jnp.sum(lagged * lagged, axis=(1, 3))
            for k, (upper, lower) in enumerate(sets):
                up, low = lax.rem(upper, blocks), lax.rem(lower, blocks)
                acc[up, w, pl.ds(low * windows * 8, windows * 8), :] += squares[k].reshape(windows * 8, LAGS)

    holder = cores * jnp.where(inner, me - COLUMNS, 2 * COLUMNS + column) + core
    crossing, holders = 2 * COLUMNS * cores, 3 * COLUMNS * cores

    def s_copy(up, low, k, there, source):
        return pltpu.make_async_remote_copy(
            src_ref=sum_out.at[up, low, k],
            dst_ref=sum_in.at[source, low],
            send_sem=s_send.at[up, low, k],
            recv_sem=s_recv.at[source, low],
            device_id={"tm": there, "chan": k},
            device_id_type=mesh_id,
        )

    def hand_over(upper, lower):
        up, low = lax.rem(upper, blocks), lax.rem(lower, blocks)
        for k in range(cores):
            result = []
            for j in range(mine):
                held = [
                    acc[up, k * mine + j, pl.ds(low * windows * 8 + i, windows, stride=8), :] for i in range(8)
                ]
                while len(held) > 1:
                    held = [one + two for one, two in zip(held[::2], held[1::2])]
                result.append(held[0])
            sum_out[up, low, k] = jnp.stack(result, axis=0).astype(bf16)

            @pl.when(jnp.logical_or(upper != me, core != k))
            def _():
                s_copy(up, low, k, upper, holder).start()

            @pl.when(jnp.logical_and(upper == me, core == k))
            def _():
                sum_in[holder, low] = sum_out[up, low, k]

    def place_of(q):
        part = jnp.where(inner, 0, q // blocks)
        i = lax.rem(q, blocks)
        far = jnp.logical_and(inner, q >= blocks)
        t = jnp.where(far, block(away, 1, i), block(here, 0, i))
        count = jnp.where(inner, jnp.where(far, blocks, 0), i + 1)
        done = jnp.where(jnp.logical_or(inner, part == 1), count, 0)
        return t, part, count, done

    def ordered(t, k):
        other = block(here, 0, k)
        return jnp.maximum(t, other), jnp.minimum(t, other)

    def step(q, carry):
        t, part, count, done = place_of(q)

        @pl.when(t == me)
        def _():
            own_copy(0, part).wait()

        @pl.when(t != me)
        def _():
            x_copy(me, 0, part, 0, t).wait_recv()

        left[t, part] = right[t, part].astype(jnp.float32)

        def two_jobs(k, inside):
            job([ordered(t, 2 * k), ordered(t, 2 * k + 1)], part)
            return inside

        lax.fori_loop(0, count // 2, two_jobs, 0)

        @pl.when(lax.rem(count, 2) == 1)
        def _():
            job([ordered(t, count - 1)], part)

        @pl.when(q == blocks)
        def _():
            pl.semaphore_wait(ready.at[2], near)

        def one_block(k, inside):
            hand_over(*ordered(t, k))
            return inside

        lax.fori_loop(0, done, one_block, 0)
        return carry

    lax.fori_loop(0, n, step, 0)

    def collect(first, last, low):
        result = None
        for source in range(first, last):
            @pl.when(jnp.logical_or(source != holder, jnp.logical_not(keeps)))
            def _():
                s_copy(0, low, 0, me, source).wait_recv()

            value = sum_in[source, low].astype(jnp.float32)
            result = value if result is None else result + value
        return result

    target = blocks * jnp.where(inner, 1, half)
    keeps = jnp.logical_and(me >= target, me < target + blocks)
    base = SPAN * windows
    for low in range(blocks):
        @pl.when(half == 1)
        def _():
            total[:, pl.ds(base + low * windows, windows), :] = collect(0, crossing, low)

        @pl.when(low <= lax.rem(me, blocks))
        def _():
            total[:, pl.ds(base + (blocks * half + low) * windows, windows), :] = collect(crossing, holders, low)

    for j in range(mine):
        out_ref[j] = total[j, pl.ds(me * windows + core * mine + j, base), :] * (1.0 / (chans * cores))

    for there, first, part, index in routes():
        @pl.when(there != me)
        def _():
            x_copy(there, first, part, index, me).wait_send()

    def sent(q, carry):
        t, _, _, done = place_of(q)

        def one_block(k, inside):
            upper, lower = ordered(t, k)
            for c in range(cores):
                @pl.when(jnp.logical_or(upper != me, core != c))
                def _():
                    s_copy(lax.rem(upper, blocks), lax.rem(lower, blocks), c, upper, holder).wait_send()

            return inside

        lax.fori_loop(0, done, one_block, 0)
        return carry

    lax.fori_loop(0, n, sent, 0)
    e_copy.wait_send()


def spread_shards(spectra, offsets, channel_group):
    windows, chans, _, freq_bins = spectra.shape
    n = lax.axis_size("tm")
    cores = lax.axis_size("chan")
    blocks = n // 2
    band = SPAN * windows
    mine = windows // cores
    dma = pltpu.SemaphoreType.DMA
    pieces = (windows, chans // PARTS // ROWS, 2, ROWS, freq_bins)
    return pl.pallas_call(
        functools.partial(kernel, n, chans, windows, freq_bins, cores),
        out_shape=pltpu.VMEM((mine, band, LAGS), jnp.float32),
        in_specs=[
            pl.BlockSpec(memory_space=pl.ANY),
            pl.BlockSpec(memory_space=pltpu.SMEM),
            pl.BlockSpec(memory_space=pltpu.VMEM),
        ],
        out_specs=pl.BlockSpec(memory_space=pltpu.VMEM),
        scratch_shapes=[
            pltpu.VMEM((windows, 2 * chans, freq_bins), jnp.bfloat16),
            pltpu.VMEM((windows * 2 * chans, freq_bins), jnp.float32),
            pltpu.VMEM((windows * GROUPS, freq_bins), jnp.float32),
            pltpu.VMEM((windows * GROUPS, freq_bins), jnp.float32),
            pltpu.VMEM((windows * GROUPS, freq_bins), jnp.float32),
            pltpu.VMEM((PARTS,) + pieces, jnp.bfloat16),
            pltpu.VMEM((n, 2) + pieces, jnp.bfloat16),
            pltpu.VMEM((n, 2) + pieces, jnp.float32),
            pltpu.VMEM((2 * freq_bins, LAGS), jnp.bfloat16),
            pltpu.VMEM((blocks, windows, blocks * windows * 8, LAGS), jnp.float32),
            pltpu.VMEM((mine, band + n * windows, LAGS), jnp.float32),
            pltpu.VMEM((blocks, blocks, cores, mine, windows, LAGS), jnp.bfloat16),
            pltpu.VMEM((3 * COLUMNS * cores, blocks, mine, windows, LAGS), jnp.bfloat16),
            dma((windows,)), dma((2,)), dma, dma, dma((n,)), dma((n, 2)),
            dma((blocks, blocks, cores)), dma((3 * COLUMNS * cores, blocks)), pltpu.SemaphoreType.REGULAR((3,)),
        ],
        compiler_params=pltpu.CompilerParams(
            collective_id=0, has_side_effects=True, vmem_limit_bytes=56 * 1024 * 1024
        ),
    )(spectra.reshape(windows, 2 * chans, freq_bins), offsets, channel_group.reshape(1, chans))


def shards(spectra, offsets, channel_group):
    windows, chans, _, freq_bins = spectra.shape
    n = lax.axis_size("tm")
    fits = (
        chans == freq_bins == LAGS == 128
        and windows == 8
        and lax.axis_size("chan") == 2
        and n == 8
    )
    return (spread_shards if fits else ring_shards)(spectra, offsets, channel_group)


def solution(mesh):
    placed = (P(("arrays", "tm"), "chan", None, None), P(("arrays", "tm")), P(("arrays", "chan")))
    return jax.shard_map(
        shards,
        mesh=mesh,
        in_specs=placed,
        out_specs=P(("arrays", "tm", "chan"), None, None),
        check_vma=False,
    )
```

```python
import functools
import math

import jax
import jax.numpy as jnp
from jax import lax
from jax.experimental import pallas as pl
from jax.experimental.pallas import tpu as pltpu
from jax.sharding import PartitionSpec as P

LAGS = 128
GROUPS = 8
SPAN = 6


epsilon = 1e-05


def shifted(value, axis, steps):
    count = lax.axis_size(axis)
    initial, last = (max(0, -steps), min(count, count - steps))
    return lax.ppermute(value, axis, [(source, source + steps) for source in range(initial, last)])


def lag_table(freq_bins, lag_count):
    frequency = jnp.arange(freq_bins, dtype=jnp.int32)[:, None]
    lag_shift = jnp.arange(lag_count, dtype=jnp.int32)[None, :] - lag_count // 2
    phase_turns = jnp.mod(frequency * lag_shift, 2 * freq_bins).astype(jnp.float32)
    phase_angle = jnp.pi * phase_turns / freq_bins
    normaliser = 1.0 / math.sqrt(freq_bins)
    lag_rows = jnp.concatenate(
        [jnp.cos(phase_angle) * normaliser, -jnp.sin(phase_angle) * normaliser], axis=0
    )
    return lag_rows.astype(jnp.bfloat16)


def align_spectra(spectra, offsets, scales):
    freq_bins = spectra.shape[3]
    frequency = jnp.arange(freq_bins, dtype=jnp.int32)[None, :]
    phase_turns = jnp.mod(offsets[:, None] * frequency, 2 * freq_bins).astype(jnp.float32)
    phase_angle = jnp.pi * phase_turns / freq_bins
    cosine = jnp.cos(phase_angle)[:, None, :]
    sine_part = jnp.sin(phase_angle)[:, None, :]
    real_part = spectra[:, :, 0, :].astype(jnp.float32)
    imag_part = spectra[:, :, 1, :].astype(jnp.float32)
    weight = scales[:, :, None]
    out_real = weight * (real_part * cosine + imag_part * sine_part)
    out_imag = weight * (imag_part * cosine - real_part * sine_part)
    return jnp.stack([out_real, out_imag], axis=2).astype(jnp.bfloat16)


def window_terms(current, band_rows, lag_rows):
    left_real = current[None, :, 0, :].astype(jnp.float32)
    left_imag = current[None, :, 1, :].astype(jnp.float32)
    right_real = band_rows[:, :, 0, :].astype(jnp.float32)
    right_imag = band_rows[:, :, 1, :].astype(jnp.float32)
    prod_real = left_real * right_real + left_imag * right_imag
    prod_imag = left_imag * right_real - left_real * right_imag
    cross_spec = jnp.stack([prod_real, prod_imag], axis=2).astype(jnp.bfloat16)
    flattened = cross_spec.reshape(band_rows.shape[0] * band_rows.shape[1], 2 * band_rows.shape[3])
    lagged = jnp.dot(flattened, lag_rows, preferred_element_type=jnp.float32)
    lagged = lagged.reshape(band_rows.shape[0], band_rows.shape[1], lag_rows.shape[1])
    return jnp.sum(lagged * lagged, axis=1)


def ring_shards(spectra, offsets, channel_group):
    windows = spectra.shape[0]
    local_chans = spectra.shape[1]
    freq_bins = spectra.shape[3]
    chan_count = lax.axis_size("chan")
    channels = local_chans * chan_count
    onehot = (channel_group[:, None] == jnp.arange(GROUPS, dtype=jnp.int32)[None, :]).astype(
        jnp.float32
    )
    chan_power = jnp.sum(jnp.square(spectra.astype(jnp.float32)), axis=(2, 3))
    partial_value = jnp.dot(chan_power, onehot, precision=lax.Precision.HIGHEST)
    group_total = lax.psum(partial_value, "chan")
    energy = group_total * (GROUPS / (freq_bins * channels))
    scales = jnp.dot(lax.rsqrt(energy + epsilon), onehot.T, precision=lax.Precision.HIGHEST)
    aligned = align_spectra(spectra, offsets, scales)
    earlier = []
    carried = aligned
    for distance in range(SPAN):
        carried = shifted(carried, "tm", 1)
        earlier.append(carried)
    buffer = jnp.concatenate(earlier[::-1] + [aligned], axis=0)
    lag_rows = lag_table(freq_bins, LAGS)
    band_len = SPAN * windows

    def one_window(window):
        current = lax.dynamic_index_in_dim(aligned, window, 0, keepdims=False)
        band_rows = lax.dynamic_slice_in_dim(buffer, window, band_len, 0)
        return window_terms(current, band_rows, lag_rows) * (1.0 / channels)

    return lax.psum_scatter(
        lax.map(
            one_window, jnp.arange(lax.axis_size("chan") * (windows // chan_count), dtype=jnp.int32)
        ).astype(jnp.bfloat16),
        "chan",
        scatter_dimension=0,
        tiled=True,
    ).astype(jnp.float32)


HIGHEST = lax.Precision.HIGHEST
ROWS = 16
COLUMNS = 2
PARTS = 4
FAR = 2


def phase_of(turns, freq_bins):
    period = 2.0 * freq_bins
    return (jnp.pi / freq_bins) * (turns - period * jnp.floor(turns / period))


def kernel(
    n, chans, windows, freq_bins, cores,
    x_ref, off_hbm, group_hbm, out_ref,
    off_ref, group_ref, local, wide, sums, tile, tile_in, al, right, left, table, acc, total, sum_out, sum_in,
    small_sem, local_sem, own_sem, e_send, e_recv, x_send, x_recv, s_send, s_recv, ready,
):
    me = lax.axis_index("tm")
    core = lax.axis_index("chan")
    levels = n // COLUMNS
    level, column = me // COLUMNS, lax.rem(me, COLUMNS)
    half = level // 2
    inner = jnp.logical_or(level == 1, level == levels - 2)
    blocks = n // 2
    mine = windows // cores
    lanes = freq_bins
    bf16 = jnp.bfloat16
    share = chans // PARTS
    tiles = share // ROWS
    mesh_id = pl.DeviceIdType.MESH

    loads = [pltpu.make_async_copy(x_ref.at[w], local.at[w], local_sem.at[w]) for w in range(windows)]
    for load in loads:
        load.start()

    barrier = pltpu.get_barrier_semaphore()
    beside = COLUMNS * level + 1 - column
    above, below = level + 1 < levels, level > 0

    def greet(sem):
        pl.semaphore_signal(sem, inc=1, device_id={"tm": beside}, device_id_type=mesh_id)

        @pl.when(above)
        def _():
            pl.semaphore_signal(sem, inc=1, device_id={"tm": me + COLUMNS}, device_id_type=mesh_id)

        @pl.when(below)
        def _():
            pl.semaphore_signal(sem, inc=1, device_id={"tm": me - COLUMNS}, device_id_type=mesh_id)

    small = [
        pltpu.make_async_copy(group_hbm, group_ref, small_sem.at[0]),
        pltpu.make_async_copy(off_hbm, off_ref, small_sem.at[1]),
    ]
    for copy in small:
        copy.start()
    near = 1 + jnp.where(above, 1, 0) + jnp.where(below, 1, 0)
    pl.semaphore_signal(barrier, inc=1, device_id={"chan": 1 - core}, device_id_type=mesh_id)
    greet(barrier)

    small[0].wait()
    frequency = lax.broadcasted_iota(jnp.int32, (freq_bins, LAGS), 0)
    shift = lax.broadcasted_iota(jnp.int32, (freq_bins, LAGS), 1) - LAGS // 2
    group_id = lax.broadcasted_iota(jnp.int32, (GROUPS, chans), 0)
    onehot = (group_id == group_ref[...]).astype(jnp.float32)
    few = onehot.astype(bf16)
    both = jnp.concatenate([few, few], axis=1)
    member = jnp.concatenate([few, few, few, few], axis=0)
    lane = lax.broadcasted_iota(jnp.int32, (windows, lanes), 1)
    row = lax.broadcasted_iota(jnp.int32, (windows, lanes), 0)

    for w in range(windows):
        loads[w].wait()
        if w == windows - 1:
            pl.semaphore_wait(barrier, near + 1)
            greet(ready.at[0])
        wide[pl.ds(w * 2 * chans, 2 * chans), :] = local[w].astype(jnp.float32)
        real = wide[pl.ds(w * 2 * chans, chans, stride=2), :]
        imag = wide[pl.ds(w * 2 * chans + 1, chans, stride=2), :]
        power = real * real + imag * imag
        high = power.astype(bf16)
        low = (power - high.astype(jnp.float32)).astype(bf16)
        sums[pl.ds(w * GROUPS, GROUPS), :] = jnp.dot(
            both, jnp.concatenate([high, low], axis=0), preferred_element_type=jnp.float32
        )
    totals = jnp.broadcast_to(jnp.sum(sums[...], axis=1, keepdims=True), sums.shape)
    tile[...] = totals
    e_copy = pltpu.make_async_remote_copy(
        src_ref=tile, dst_ref=tile_in, send_sem=e_send, recv_sem=e_recv,
        device_id={"chan": 1 - core}, device_id_type=mesh_id,
    )
    e_copy.start()

    angle = phase_of((frequency * shift).astype(jnp.float32), freq_bins)
    normaliser = 1.0 / math.sqrt(freq_bins)
    table[pl.ds(0, freq_bins), :] = (jnp.cos(angle) * normaliser).astype(bf16)
    table[pl.ds(freq_bins, freq_bins), :] = (-jnp.sin(angle) * normaliser).astype(bf16)
    small[1].wait()
    starts = jnp.zeros((windows, lanes), jnp.float32)
    for w in range(windows):
        starts = jnp.where(row == w, off_ref[w].astype(jnp.float32), starts)
    theta = phase_of(lane.astype(jnp.float32) * starts, freq_bins)
    cosine = jnp.cos(theta)
    sine = jnp.sin(theta)
    acc[...] = jnp.zeros_like(acc)
    total[:, pl.ds(0, SPAN * windows), :] = jnp.zeros((mine, SPAN * windows, LAGS), jnp.float32)

    pl.semaphore_wait(ready.at[0], near)
    greet(ready.at[1])
    e_copy.wait_recv()
    energy = (totals + tile_in[...]) * (GROUPS / (freq_bins * chans * cores))
    scales = lax.rsqrt(energy + epsilon)

    for w in range(windows):
        factor = scales[w * GROUPS : (w + 1) * GROUPS]
        turn = jnp.concatenate([factor * cosine[w : w + 1], factor * sine[w : w + 1]], axis=1)
        top = turn.astype(bf16)
        rest = turn - top.astype(jnp.float32)
        middle = rest.astype(bf16)
        bottom = (rest - middle.astype(jnp.float32)).astype(bf16)
        pieces = jnp.concatenate([top, middle, bottom, jnp.zeros_like(top)], axis=0)
        factors = lax.dot_general(
            member, pieces, (((0,), (0,)), ((), ())), preferred_element_type=jnp.float32
        )
        real = wide[pl.ds(w * 2 * chans, chans, stride=2), :]
        imag = wide[pl.ds(w * 2 * chans + 1, chans, stride=2), :]
        turn_cos, turn_sin = factors[:, :lanes], factors[:, lanes:]
        out = (real * turn_cos + imag * turn_sin, imag * turn_cos - real * turn_sin)
        for r in range(2):
            al[:, w, :, r] = out[r].astype(bf16).reshape(PARTS, tiles, ROWS, freq_bins)

    def routes():
        def inside(own, flip):
            place = COLUMNS * (half if own else 1 - half) + lax.rem(column + core + flip, 2)
            return COLUMNS + place, place, 0, 2 * (1 - own) + flip

        yield inside(1, 0)
        yield inside(1, 1)
        yield inside(0, 0)
        yield inside(0, 1)
        for part in range(2):
            for flip in range(COLUMNS):
                place = lax.rem(column + core + flip, 2)
                yield (n - COLUMNS) * half + place, 2 * place + part, part, 4 + 2 * part + flip

    def x_copy(there, first, part, index, source):
        return pltpu.make_async_remote_copy(
            src_ref=al.at[first],
            dst_ref=right.at[source, part],
            send_sem=x_send.at[index],
            recv_sem=x_recv.at[source, part],
            device_id={"tm": there},
            device_id_type=mesh_id,
        )

    def own_copy(first, part):
        return pltpu.make_async_copy(al.at[first], right.at[me, part], own_sem.at[part])

    for there, first, part, index in routes():
        if index == FAR:
            @pl.when(jnp.logical_not(inner))
            def _():
                pl.semaphore_wait(ready.at[1], near)

        @pl.when(there == me)
        def _():
            own_copy(first, part).start()

        @pl.when(there != me)
        def _():
            x_copy(there, first, part, index, me).start()

    @pl.when(inner)
    def _():
        pl.semaphore_wait(ready.at[1], near)

    greet(ready.at[2])

    bit = lax.rem(level, 2)

    def block(base, flip, k):
        turned = core * jnp.maximum(flip, k // 2)
        return base + COLUMNS * lax.rem(bit + flip + k // 2, 2) + lax.rem(column + turned + lax.rem(k, 2), 2)

    here, away = blocks * half, blocks * (1 - half)

    def job(sets, part):
        for w in range(windows):
            rows = []
            for upper, lower in sets:
                for i in range(tiles):
                    left_real = left[upper, part, w, i, 0].astype(bf16)
                    left_imag = left[upper, part, w, i, 1].astype(bf16)
                    for v in range(windows):
                        right_real = right[lower, part, v, i, 0]
                        right_imag = right[lower, part, v, i, 1]
                        rows.append(
                            jnp.concatenate(
                                [
                                    left_real * right_real + left_imag * right_imag,
                                    left_imag * right_real - left_real * right_imag,
                                ],
                                axis=1,
                            )
                        )
            lagged = jnp.dot(jnp.concatenate(rows, axis=0), table[...], preferred_element_type=jnp.float32)
            lagged = lagged.reshape(len(sets), tiles, windows, ROWS // 8, 8, LAGS)
            squares = jnp.sum(lagged * lagged, axis=(1, 3))
            for k, (upper, lower) in enumerate(sets):
                up, low = lax.rem(upper, blocks), lax.rem(lower, blocks)
                acc[up, w, pl.ds(low * windows * 8, windows * 8), :] += squares[k].reshape(windows * 8, LAGS)

    holder = cores * jnp.where(inner, me - COLUMNS, 2 * COLUMNS + column) + core
    crossing, holders = 2 * COLUMNS * cores, 3 * COLUMNS * cores

    def s_copy(up, low, k, there, source):
        return pltpu.make_async_remote_copy(
            src_ref=sum_out.at[up, low, k],
            dst_ref=sum_in.at[source, low],
            send_sem=s_send.at[up, low, k],
            recv_sem=s_recv.at[source, low],
            device_id={"tm": there, "chan": k},
            device_id_type=mesh_id,
        )

    def hand_over(upper, lower):
        up, low = lax.rem(upper, blocks), lax.rem(lower, blocks)
        for k in range(cores):
            result = []
            for j in range(mine):
                held = [
                    acc[up, k * mine + j, pl.ds(low * windows * 8 + i, windows, stride=8), :] for i in range(8)
                ]
                while len(held) > 1:
                    held = [one + two for one, two in zip(held[::2], held[1::2])]
                result.append(held[0])
            sum_out[up, low, k] = jnp.stack(result, axis=0).astype(bf16)

            @pl.when(jnp.logical_or(upper != me, core != k))
            def _():
                s_copy(up, low, k, upper, holder).start()

            @pl.when(jnp.logical_and(upper == me, core == k))
            def _():
                sum_in[holder, low] = sum_out[up, low, k]

    def place_of(q):
        part = jnp.where(inner, 0, q // blocks)
        i = lax.rem(q, blocks)
        far = jnp.logical_and(inner, q >= blocks)
        t = jnp.where(far, block(away, 1, i), block(here, 0, i))
        count = jnp.where(inner, jnp.where(far, blocks, 0), i + 1)
        done = jnp.where(jnp.logical_or(inner, part == 1), count, 0)
        return t, part, count, done

    def ordered(t, k):
        other = block(here, 0, k)
        return jnp.maximum(t, other), jnp.minimum(t, other)

    def step(q, carry):
        t, part, count, done = place_of(q)

        @pl.when(t == me)
        def _():
            own_copy(0, part).wait()

        @pl.when(t != me)
        def _():
            x_copy(me, 0, part, 0, t).wait_recv()

        left[t, part] = right[t, part].astype(jnp.float32)

        @pl.when(q == 1)
        def _():
            pl.semaphore_wait(ready.at[2], near)

        finished = done > 0

        def two_jobs(k, inside):
            sets = [ordered(t, 2 * k), ordered(t, 2 * k + 1)]
            job(sets, part)

            @pl.when(finished)
            def _():
                for upper, lower in sets:
                    hand_over(upper, lower)

            return inside

        lax.fori_loop(0, count // 2, two_jobs, 0)

        @pl.when(lax.rem(count, 2) == 1)
        def _():
            upper, lower = ordered(t, count - 1)
            job([(upper, lower)], part)

            @pl.when(finished)
            def _():
                hand_over(upper, lower)

        return carry

    lax.fori_loop(0, n, step, 0)

    def collect(first, last, low):
        result = None
        for source in range(first, last):
            @pl.when(jnp.logical_or(source != holder, jnp.logical_not(keeps)))
            def _():
                s_copy(0, low, 0, me, source).wait_recv()

            value = sum_in[source, low].astype(jnp.float32)
            result = value if result is None else result + value
        return result

    target = blocks * jnp.where(inner, 1, half)
    keeps = jnp.logical_and(me >= target, me < target + blocks)
    base = SPAN * windows
    for low in range(blocks):
        @pl.when(half == 1)
        def _():
            total[:, pl.ds(base + low * windows, windows), :] = collect(0, crossing, low)

        @pl.when(low <= lax.rem(me, blocks))
        def _():
            total[:, pl.ds(base + (blocks * half + low) * windows, windows), :] = collect(crossing, holders, low)

    for j in range(mine):
        out_ref[j] = total[j, pl.ds(me * windows + core * mine + j, base), :] * (1.0 / (chans * cores))

    for there, first, part, index in routes():
        @pl.when(there != me)
        def _():
            x_copy(there, first, part, index, me).wait_send()

    def sent(q, carry):
        t, _, _, done = place_of(q)

        def one_block(k, inside):
            upper, lower = ordered(t, k)
            for c in range(cores):
                @pl.when(jnp.logical_or(upper != me, core != c))
                def _():
                    s_copy(lax.rem(upper, blocks), lax.rem(lower, blocks), c, upper, holder).wait_send()

            return inside

        lax.fori_loop(0, done, one_block, 0)
        return carry

    lax.fori_loop(0, n, sent, 0)
    e_copy.wait_send()


def spread_shards(spectra, offsets, channel_group):
    windows, chans, _, freq_bins = spectra.shape
    n = lax.axis_size("tm")
    cores = lax.axis_size("chan")
    blocks = n // 2
    band = SPAN * windows
    mine = windows // cores
    dma = pltpu.SemaphoreType.DMA
    pieces = (windows, chans // PARTS // ROWS, 2, ROWS, freq_bins)
    return pl.pallas_call(
        functools.partial(kernel, n, chans, windows, freq_bins, cores),
        out_shape=pltpu.VMEM((mine, band, LAGS), jnp.float32),
        in_specs=[
            pl.BlockSpec(memory_space=pl.ANY),
            pl.BlockSpec(memory_space=pl.ANY),
            pl.BlockSpec(memory_space=pl.ANY),
        ],
        out_specs=pl.BlockSpec(memory_space=pltpu.VMEM),
        scratch_shapes=[
            pltpu.SMEM((windows,), jnp.int32),
            pltpu.VMEM((1, chans), jnp.int32),
            pltpu.VMEM((windows, 2 * chans, freq_bins), jnp.bfloat16),
            pltpu.VMEM((windows * 2 * chans, freq_bins), jnp.float32),
            pltpu.VMEM((windows * GROUPS, freq_bins), jnp.float32),
            pltpu.VMEM((windows * GROUPS, freq_bins), jnp.float32),
            pltpu.VMEM((windows * GROUPS, freq_bins), jnp.float32),
            pltpu.VMEM((PARTS,) + pieces, jnp.bfloat16),
            pltpu.VMEM((n, 2) + pieces, jnp.bfloat16),
            pltpu.VMEM((n, 2) + pieces, jnp.float32),
            pltpu.VMEM((2 * freq_bins, LAGS), jnp.bfloat16),
            pltpu.VMEM((blocks, windows, blocks * windows * 8, LAGS), jnp.float32),
            pltpu.VMEM((mine, band + n * windows, LAGS), jnp.float32),
            pltpu.VMEM((blocks, blocks, cores, mine, windows, LAGS), jnp.bfloat16),
            pltpu.VMEM((3 * COLUMNS * cores, blocks, mine, windows, LAGS), jnp.bfloat16),
            dma((2,)), dma((windows,)), dma((2,)), dma, dma, dma((n,)), dma((n, 2)),
            dma((blocks, blocks, cores)), dma((3 * COLUMNS * cores, blocks)), pltpu.SemaphoreType.REGULAR((3,)),
        ],
        compiler_params=pltpu.CompilerParams(
            collective_id=0, has_side_effects=True, vmem_limit_bytes=56 * 1024 * 1024
        ),
    )(spectra.reshape(windows, 2 * chans, freq_bins), offsets, channel_group.reshape(1, chans))


def shards(spectra, offsets, channel_group):
    windows, chans, _, freq_bins = spectra.shape
    n = lax.axis_size("tm")
    fits = (
        chans == freq_bins == LAGS == 128
        and windows == 8
        and lax.axis_size("chan") == 2
        and n == 8
    )
    return (spread_shards if fits else ring_shards)(spectra, offsets, channel_group)


def solution(mesh):
    placed = (P(("arrays", "tm"), "chan", None, None), P(("arrays", "tm")), P(("arrays", "chan")))
    return jax.shard_map(
        shards,
        mesh=mesh,
        in_specs=placed,
        out_specs=P(("arrays", "tm", "chan"), None, None),
        check_vma=False,
    )
```

```python
import functools
import math

import jax
import jax.numpy as jnp
from jax import lax
from jax.experimental import pallas as pl
from jax.experimental.pallas import tpu as pltpu
from jax.sharding import PartitionSpec as P

LAGS = 128
GROUPS = 8
SPAN = 6


epsilon = 1e-05


def shifted(value, axis, steps):
    count = lax.axis_size(axis)
    initial, last = (max(0, -steps), min(count, count - steps))
    return lax.ppermute(value, axis, [(source, source + steps) for source in range(initial, last)])


def lag_table(freq_bins, lag_count):
    frequency = jnp.arange(freq_bins, dtype=jnp.int32)[:, None]
    lag_shift = jnp.arange(lag_count, dtype=jnp.int32)[None, :] - lag_count // 2
    phase_turns = jnp.mod(frequency * lag_shift, 2 * freq_bins).astype(jnp.float32)
    phase_angle = jnp.pi * phase_turns / freq_bins
    normaliser = 1.0 / math.sqrt(freq_bins)
    lag_rows = jnp.concatenate(
        [jnp.cos(phase_angle) * normaliser, -jnp.sin(phase_angle) * normaliser], axis=0
    )
    return lag_rows.astype(jnp.bfloat16)


def align_spectra(spectra, offsets, scales):
    freq_bins = spectra.shape[3]
    frequency = jnp.arange(freq_bins, dtype=jnp.int32)[None, :]
    phase_turns = jnp.mod(offsets[:, None] * frequency, 2 * freq_bins).astype(jnp.float32)
    phase_angle = jnp.pi * phase_turns / freq_bins
    cosine = jnp.cos(phase_angle)[:, None, :]
    sine_part = jnp.sin(phase_angle)[:, None, :]
    real_part = spectra[:, :, 0, :].astype(jnp.float32)
    imag_part = spectra[:, :, 1, :].astype(jnp.float32)
    weight = scales[:, :, None]
    out_real = weight * (real_part * cosine + imag_part * sine_part)
    out_imag = weight * (imag_part * cosine - real_part * sine_part)
    return jnp.stack([out_real, out_imag], axis=2).astype(jnp.bfloat16)


def window_terms(current, band_rows, lag_rows):
    left_real = current[None, :, 0, :].astype(jnp.float32)
    left_imag = current[None, :, 1, :].astype(jnp.float32)
    right_real = band_rows[:, :, 0, :].astype(jnp.float32)
    right_imag = band_rows[:, :, 1, :].astype(jnp.float32)
    prod_real = left_real * right_real + left_imag * right_imag
    prod_imag = left_imag * right_real - left_real * right_imag
    cross_spec = jnp.stack([prod_real, prod_imag], axis=2).astype(jnp.bfloat16)
    flattened = cross_spec.reshape(band_rows.shape[0] * band_rows.shape[1], 2 * band_rows.shape[3])
    lagged = jnp.dot(flattened, lag_rows, preferred_element_type=jnp.float32)
    lagged = lagged.reshape(band_rows.shape[0], band_rows.shape[1], lag_rows.shape[1])
    return jnp.sum(lagged * lagged, axis=1)


def ring_shards(spectra, offsets, channel_group):
    windows = spectra.shape[0]
    local_chans = spectra.shape[1]
    freq_bins = spectra.shape[3]
    chan_count = lax.axis_size("chan")
    channels = local_chans * chan_count
    onehot = (channel_group[:, None] == jnp.arange(GROUPS, dtype=jnp.int32)[None, :]).astype(
        jnp.float32
    )
    chan_power = jnp.sum(jnp.square(spectra.astype(jnp.float32)), axis=(2, 3))
    partial_value = jnp.dot(chan_power, onehot, precision=lax.Precision.HIGHEST)
    group_total = lax.psum(partial_value, "chan")
    energy = group_total * (GROUPS / (freq_bins * channels))
    scales = jnp.dot(lax.rsqrt(energy + epsilon), onehot.T, precision=lax.Precision.HIGHEST)
    aligned = align_spectra(spectra, offsets, scales)
    earlier = []
    carried = aligned
    for distance in range(SPAN):
        carried = shifted(carried, "tm", 1)
        earlier.append(carried)
    buffer = jnp.concatenate(earlier[::-1] + [aligned], axis=0)
    lag_rows = lag_table(freq_bins, LAGS)
    band_len = SPAN * windows

    def one_window(window):
        current = lax.dynamic_index_in_dim(aligned, window, 0, keepdims=False)
        band_rows = lax.dynamic_slice_in_dim(buffer, window, band_len, 0)
        return window_terms(current, band_rows, lag_rows) * (1.0 / channels)

    return lax.psum_scatter(
        lax.map(
            one_window, jnp.arange(lax.axis_size("chan") * (windows // chan_count), dtype=jnp.int32)
        ).astype(jnp.bfloat16),
        "chan",
        scatter_dimension=0,
        tiled=True,
    ).astype(jnp.float32)


HIGHEST = lax.Precision.HIGHEST
ROWS = 16
FAR = 2
COLUMNS = 2
PARTS = 4


def phase_of(turns, freq_bins):
    period = 2.0 * freq_bins
    return (jnp.pi / freq_bins) * (turns - period * jnp.floor(turns / period))


def kernel(
    n, chans, windows, freq_bins, cores,
    x_ref, off_hbm, group_hbm, out_ref,
    off_ref, group_ref, local, wide, sums, tile, tile_in, al, right, left, table, acc, total, sum_out, sum_in,
    small_sem, local_sem, own_sem, e_send, e_recv, x_send, x_recv, s_send, s_recv, ready,
):
    me = lax.axis_index("tm")
    core = lax.axis_index("chan")
    levels = n // COLUMNS
    level, column = me // COLUMNS, lax.rem(me, COLUMNS)
    half = level // 2
    inner = jnp.logical_or(level == 1, level == levels - 2)
    blocks = n // 2
    mine = windows // cores
    lanes = freq_bins
    bf16 = jnp.bfloat16
    share = chans // PARTS
    tiles = share // ROWS
    mesh_id = pl.DeviceIdType.MESH

    loads = [pltpu.make_async_copy(x_ref.at[w], local.at[w], local_sem.at[w]) for w in range(windows)]
    for load in loads:
        load.start()

    barrier = pltpu.get_barrier_semaphore()
    beside = COLUMNS * level + 1 - column
    above, below = level + 1 < levels, level > 0

    def greet(sem):
        pl.semaphore_signal(sem, inc=1, device_id={"tm": beside}, device_id_type=mesh_id)

        @pl.when(above)
        def _():
            pl.semaphore_signal(sem, inc=1, device_id={"tm": me + COLUMNS}, device_id_type=mesh_id)

        @pl.when(below)
        def _():
            pl.semaphore_signal(sem, inc=1, device_id={"tm": me - COLUMNS}, device_id_type=mesh_id)

    small = [
        pltpu.make_async_copy(group_hbm, group_ref, small_sem.at[0]),
        pltpu.make_async_copy(off_hbm, off_ref, small_sem.at[1]),
    ]
    for copy in small:
        copy.start()
    near = 1 + jnp.where(above, 1, 0) + jnp.where(below, 1, 0)
    pl.semaphore_signal(barrier, inc=1, device_id={"chan": 1 - core}, device_id_type=mesh_id)
    greet(barrier)

    small[0].wait()
    frequency = lax.broadcasted_iota(jnp.int32, (freq_bins, LAGS), 0)
    shift = lax.broadcasted_iota(jnp.int32, (freq_bins, LAGS), 1) - LAGS // 2
    group_id = lax.broadcasted_iota(jnp.int32, (GROUPS, chans), 0)
    onehot = (group_id == group_ref[...]).astype(jnp.float32)
    few = onehot.astype(bf16)
    both = jnp.concatenate([few, few], axis=1)
    member = jnp.concatenate([few, few, few, few], axis=0)
    lane = lax.broadcasted_iota(jnp.int32, (windows, lanes), 1)
    row = lax.broadcasted_iota(jnp.int32, (windows, lanes), 0)

    for w in range(windows):
        loads[w].wait()
        if w == windows - 1:
            pl.semaphore_wait(barrier, near + 1)
            greet(ready.at[0])
        wide[pl.ds(w * 2 * chans, 2 * chans), :] = local[w].astype(jnp.float32)
        real = wide[pl.ds(w * 2 * chans, chans, stride=2), :]
        imag = wide[pl.ds(w * 2 * chans + 1, chans, stride=2), :]
        power = real * real + imag * imag
        high = power.astype(bf16)
        low = (power - high.astype(jnp.float32)).astype(bf16)
        sums[pl.ds(w * GROUPS, GROUPS), :] = jnp.dot(
            both, jnp.concatenate([high, low], axis=0), preferred_element_type=jnp.float32
        )
    totals = jnp.broadcast_to(jnp.sum(sums[...], axis=1, keepdims=True), sums.shape)
    tile[...] = totals
    e_copy = pltpu.make_async_remote_copy(
        src_ref=tile, dst_ref=tile_in, send_sem=e_send, recv_sem=e_recv,
        device_id={"chan": 1 - core}, device_id_type=mesh_id,
    )
    e_copy.start()

    angle = phase_of((frequency * shift).astype(jnp.float32), freq_bins)
    normaliser = 1.0 / math.sqrt(freq_bins)
    table[pl.ds(0, freq_bins), :] = (jnp.cos(angle) * normaliser).astype(bf16)
    table[pl.ds(freq_bins, freq_bins), :] = (-jnp.sin(angle) * normaliser).astype(bf16)
    small[1].wait()
    starts = jnp.zeros((windows, lanes), jnp.float32)
    for w in range(windows):
        starts = jnp.where(row == w, off_ref[w].astype(jnp.float32), starts)
    theta = phase_of(lane.astype(jnp.float32) * starts, freq_bins)
    cosine = jnp.cos(theta)
    sine = jnp.sin(theta)
    acc[...] = jnp.zeros_like(acc)
    total[:, pl.ds(0, SPAN * windows), :] = jnp.zeros((mine, SPAN * windows, LAGS), jnp.float32)

    pl.semaphore_wait(ready.at[0], near)
    greet(ready.at[1])
    e_copy.wait_recv()
    energy = (totals + tile_in[...]) * (GROUPS / (freq_bins * chans * cores))
    scales = lax.rsqrt(energy + epsilon)

    for w in range(windows):
        factor = scales[w * GROUPS : (w + 1) * GROUPS]
        turn = jnp.concatenate([factor * cosine[w : w + 1], factor * sine[w : w + 1]], axis=1)
        top = turn.astype(bf16)
        rest = turn - top.astype(jnp.float32)
        middle = rest.astype(bf16)
        bottom = (rest - middle.astype(jnp.float32)).astype(bf16)
        pieces = jnp.concatenate([top, middle, bottom, jnp.zeros_like(top)], axis=0)
        factors = lax.dot_general(
            member, pieces, (((0,), (0,)), ((), ())), preferred_element_type=jnp.float32
        )
        real = wide[pl.ds(w * 2 * chans, chans, stride=2), :]
        imag = wide[pl.ds(w * 2 * chans + 1, chans, stride=2), :]
        turn_cos, turn_sin = factors[:, :lanes], factors[:, lanes:]
        out = (real * turn_cos + imag * turn_sin, imag * turn_cos - real * turn_sin)
        for r in range(2):
            al[:, w, :, r] = out[r].astype(bf16).reshape(PARTS, tiles, ROWS, freq_bins)

    def routes():
        def inside(own, flip):
            place = COLUMNS * (half if own else 1 - half) + lax.rem(column + core + flip, 2)
            return COLUMNS + place, place, 0, 2 * (1 - own) + flip

        yield inside(1, 0)
        yield inside(1, 1)
        yield inside(0, 0)
        yield inside(0, 1)
        for part in range(2):
            for flip in range(COLUMNS):
                place = lax.rem(column + core + flip, 2)
                yield (n - COLUMNS) * half + place, 2 * place + part, part, 4 + 2 * part + flip

    def x_copy(there, first, part, index, source):
        return pltpu.make_async_remote_copy(
            src_ref=al.at[first],
            dst_ref=right.at[source, part],
            send_sem=x_send.at[index],
            recv_sem=x_recv.at[source, part],
            device_id={"tm": there},
            device_id_type=mesh_id,
        )

    def own_copy(first, part):
        return pltpu.make_async_copy(al.at[first], right.at[me, part], own_sem.at[part])

    ways = list(routes())

    def send(index):
        there, first, part, index = ways[index]

        @pl.when(there == me)
        def _():
            own_copy(first, part).start()

        @pl.when(there != me)
        def _():
            x_copy(there, first, part, index, me).start()

    @pl.when(inner)
    def _():
        for index in (0, 1, 4, 5, 6, 7, 2, 3):
            send(index)

    @pl.when(jnp.logical_not(inner))
    def _():
        for index in (0, 1, 4, 5, 6, 7, 2, 3):
            if index == FAR:
                pl.semaphore_wait(ready.at[1], near)
            send(index)

    @pl.when(inner)
    def _():
        pl.semaphore_wait(ready.at[1], near)

    greet(ready.at[2])

    bit = lax.rem(level, 2)

    def block(base, flip, k):
        turned = core * jnp.maximum(flip, k // 2)
        return base + COLUMNS * lax.rem(bit + flip + k // 2, 2) + lax.rem(column + turned + lax.rem(k, 2), 2)

    here, away = blocks * half, blocks * (1 - half)

    def job(sets, part):
        for w in range(windows):
            rows = []
            for upper, lower in sets:
                for i in range(tiles):
                    left_real = left[upper, part, w, i, 0].astype(bf16)
                    left_imag = left[upper, part, w, i, 1].astype(bf16)
                    for v in range(windows):
                        right_real = right[lower, part, v, i, 0]
                        right_imag = right[lower, part, v, i, 1]
                        rows.append(
                            jnp.concatenate(
                                [
                                    left_real * right_real + left_imag * right_imag,
                                    left_imag * right_real - left_real * right_imag,
                                ],
                                axis=1,
                            )
                        )
            lagged = jnp.dot(jnp.concatenate(rows, axis=0), table[...], preferred_element_type=jnp.float32)
            lagged = lagged.reshape(len(sets), tiles, windows, ROWS // 8, 8, LAGS)
            squares = jnp.sum(lagged * lagged, axis=(1, 3))
            for k, (upper, lower) in enumerate(sets):
                up, low = lax.rem(upper, blocks), lax.rem(lower, blocks)
                acc[up, w, pl.ds(low * windows * 8, windows * 8), :] += squares[k].reshape(windows * 8, LAGS)

    holder = cores * jnp.where(inner, me - COLUMNS, 2 * COLUMNS + column) + core
    crossing, holders = 2 * COLUMNS * cores, 3 * COLUMNS * cores

    def s_copy(up, low, k, there, source):
        return pltpu.make_async_remote_copy(
            src_ref=sum_out.at[up, low, k],
            dst_ref=sum_in.at[source, low],
            send_sem=s_send.at[up, low, k],
            recv_sem=s_recv.at[source, low],
            device_id={"tm": there, "chan": k},
            device_id_type=mesh_id,
        )

    def hand_over(upper, lower):
        up, low = lax.rem(upper, blocks), lax.rem(lower, blocks)
        for k in range(cores):
            result = []
            for j in range(mine):
                held = [
                    acc[up, k * mine + j, pl.ds(low * windows * 8 + i, windows, stride=8), :] for i in range(8)
                ]
                while len(held) > 1:
                    held = [one + two for one, two in zip(held[::2], held[1::2])]
                result.append(held[0])
            sum_out[up, low, k] = jnp.stack(result, axis=0).astype(bf16)

            @pl.when(jnp.logical_or(upper != me, core != k))
            def _():
                s_copy(up, low, k, upper, holder).start()

            @pl.when(jnp.logical_and(upper == me, core == k))
            def _():
                sum_in[holder, low] = sum_out[up, low, k]

    def place_of(q):
        part = jnp.where(inner, 0, q // blocks)
        i = lax.rem(q, blocks)
        far = jnp.logical_and(inner, q >= blocks)
        t = jnp.where(far, block(away, 1, i), block(here, 0, i))
        count = jnp.where(inner, jnp.where(far, blocks, 0), i + 1)
        done = jnp.where(jnp.logical_or(inner, part == 1), count, 0)
        return t, part, count, done

    def ordered(t, k):
        other = block(here, 0, k)
        return jnp.maximum(t, other), jnp.minimum(t, other)

    def step(q, carry):
        t, part, count, done = place_of(q)

        @pl.when(t == me)
        def _():
            own_copy(0, part).wait()

        @pl.when(t != me)
        def _():
            x_copy(me, 0, part, 0, t).wait_recv()

        left[t, part] = right[t, part].astype(jnp.float32)

        @pl.when(q == 1)
        def _():
            pl.semaphore_wait(ready.at[2], near)

        finished = done > 0

        def two_jobs(k, inside):
            sets = [ordered(t, 2 * k), ordered(t, 2 * k + 1)]
            job(sets, part)

            @pl.when(finished)
            def _():
                for upper, lower in sets:
                    hand_over(upper, lower)

            return inside

        lax.fori_loop(0, count // 2, two_jobs, 0)

        @pl.when(lax.rem(count, 2) == 1)
        def _():
            upper, lower = ordered(t, count - 1)
            job([(upper, lower)], part)

            @pl.when(finished)
            def _():
                hand_over(upper, lower)

        return carry

    lax.fori_loop(0, n, step, 0)

    def collect(first, last, low):
        result = None
        for source in range(first, last):
            @pl.when(jnp.logical_or(source != holder, jnp.logical_not(keeps)))
            def _():
                s_copy(0, low, 0, me, source).wait_recv()

            value = sum_in[source, low].astype(jnp.float32)
            result = value if result is None else result + value
        return result

    target = blocks * jnp.where(inner, 1, half)
    keeps = jnp.logical_and(me >= target, me < target + blocks)
    base = SPAN * windows
    for low in range(blocks):
        @pl.when(low <= lax.rem(me, blocks))
        def _():
            total[:, pl.ds(base + (blocks * half + low) * windows, windows), :] = collect(crossing, holders, low)

    for low in range(blocks):
        @pl.when(half == 1)
        def _():
            total[:, pl.ds(base + low * windows, windows), :] = collect(crossing // 2, crossing, low)

    for low in range(blocks):
        @pl.when(half == 1)
        def _():
            total[:, pl.ds(base + low * windows, windows), :] += collect(0, crossing // 2, low)

    for j in range(mine):
        out_ref[j] = total[j, pl.ds(me * windows + core * mine + j, base), :] * (1.0 / (chans * cores))

    for there, first, part, index in ways:
        @pl.when(there != me)
        def _():
            x_copy(there, first, part, index, me).wait_send()

    def sent(q, carry):
        t, _, _, done = place_of(q)

        def one_block(k, inside):
            upper, lower = ordered(t, k)
            for c in range(cores):
                @pl.when(jnp.logical_or(upper != me, core != c))
                def _():
                    s_copy(lax.rem(upper, blocks), lax.rem(lower, blocks), c, upper, holder).wait_send()

            return inside

        lax.fori_loop(0, done, one_block, 0)
        return carry

    lax.fori_loop(0, n, sent, 0)
    e_copy.wait_send()


def spread_shards(spectra, offsets, channel_group):
    windows, chans, _, freq_bins = spectra.shape
    n = lax.axis_size("tm")
    cores = lax.axis_size("chan")
    blocks = n // 2
    band = SPAN * windows
    mine = windows // cores
    dma = pltpu.SemaphoreType.DMA
    pieces = (windows, chans // PARTS // ROWS, 2, ROWS, freq_bins)
    return pl.pallas_call(
        functools.partial(kernel, n, chans, windows, freq_bins, cores),
        out_shape=pltpu.VMEM((mine, band, LAGS), jnp.float32),
        in_specs=[
            pl.BlockSpec(memory_space=pl.ANY),
            pl.BlockSpec(memory_space=pl.ANY),
            pl.BlockSpec(memory_space=pl.ANY),
        ],
        out_specs=pl.BlockSpec(memory_space=pltpu.VMEM),
        scratch_shapes=[
            pltpu.SMEM((windows,), jnp.int32),
            pltpu.VMEM((1, chans), jnp.int32),
            pltpu.VMEM((windows, 2 * chans, freq_bins), jnp.bfloat16),
            pltpu.VMEM((windows * 2 * chans, freq_bins), jnp.float32),
            pltpu.VMEM((windows * GROUPS, freq_bins), jnp.float32),
            pltpu.VMEM((windows * GROUPS, freq_bins), jnp.float32),
            pltpu.VMEM((windows * GROUPS, freq_bins), jnp.float32),
            pltpu.VMEM((PARTS,) + pieces, jnp.bfloat16),
            pltpu.VMEM((n, 2) + pieces, jnp.bfloat16),
            pltpu.VMEM((n, 2) + pieces, jnp.float32),
            pltpu.VMEM((2 * freq_bins, LAGS), jnp.bfloat16),
            pltpu.VMEM((blocks, windows, blocks * windows * 8, LAGS), jnp.float32),
            pltpu.VMEM((mine, band + n * windows, LAGS), jnp.float32),
            pltpu.VMEM((blocks, blocks, cores, mine, windows, LAGS), jnp.bfloat16),
            pltpu.VMEM((3 * COLUMNS * cores, blocks, mine, windows, LAGS), jnp.bfloat16),
            dma((2,)), dma((windows,)), dma((2,)), dma, dma, dma((n,)), dma((n, 2)),
            dma((blocks, blocks, cores)), dma((3 * COLUMNS * cores, blocks)), pltpu.SemaphoreType.REGULAR((3,)),
        ],
        compiler_params=pltpu.CompilerParams(
            collective_id=0, has_side_effects=True, vmem_limit_bytes=56 * 1024 * 1024
        ),
    )(spectra.reshape(windows, 2 * chans, freq_bins), offsets, channel_group.reshape(1, chans))


def shards(spectra, offsets, channel_group):
    windows, chans, _, freq_bins = spectra.shape
    n = lax.axis_size("tm")
    fits = (
        chans == freq_bins == LAGS == 128
        and windows == 8
        and lax.axis_size("chan") == 2
        and n == 8
    )
    return (spread_shards if fits else ring_shards)(spectra, offsets, channel_group)


def solution(mesh):
    placed = (P(("arrays", "tm"), "chan", None, None), P(("arrays", "tm")), P(("arrays", "chan")))
    return jax.shard_map(
        shards,
        mesh=mesh,
        in_specs=placed,
        out_specs=P(("arrays", "tm", "chan"), None, None),
        check_vma=False,
    )
```

```python
import functools
import math

import jax
import jax.numpy as jnp
from jax import lax
from jax.experimental import pallas as pl
from jax.experimental.pallas import tpu as pltpu
from jax.sharding import PartitionSpec as P

LAGS = 128
GROUPS = 8
SPAN = 6


epsilon = 1e-05


def shifted(value, axis, steps):
    count = lax.axis_size(axis)
    initial, last = (max(0, -steps), min(count, count - steps))
    return lax.ppermute(value, axis, [(source, source + steps) for source in range(initial, last)])


def lag_table(freq_bins, lag_count):
    frequency = jnp.arange(freq_bins, dtype=jnp.int32)[:, None]
    lag_shift = jnp.arange(lag_count, dtype=jnp.int32)[None, :] - lag_count // 2
    phase_turns = jnp.mod(frequency * lag_shift, 2 * freq_bins).astype(jnp.float32)
    phase_angle = jnp.pi * phase_turns / freq_bins
    normaliser = 1.0 / math.sqrt(freq_bins)
    lag_rows = jnp.concatenate(
        [jnp.cos(phase_angle) * normaliser, -jnp.sin(phase_angle) * normaliser], axis=0
    )
    return lag_rows.astype(jnp.bfloat16)


def align_spectra(spectra, offsets, scales):
    freq_bins = spectra.shape[3]
    frequency = jnp.arange(freq_bins, dtype=jnp.int32)[None, :]
    phase_turns = jnp.mod(offsets[:, None] * frequency, 2 * freq_bins).astype(jnp.float32)
    phase_angle = jnp.pi * phase_turns / freq_bins
    cosine = jnp.cos(phase_angle)[:, None, :]
    sine_part = jnp.sin(phase_angle)[:, None, :]
    real_part = spectra[:, :, 0, :].astype(jnp.float32)
    imag_part = spectra[:, :, 1, :].astype(jnp.float32)
    weight = scales[:, :, None]
    out_real = weight * (real_part * cosine + imag_part * sine_part)
    out_imag = weight * (imag_part * cosine - real_part * sine_part)
    return jnp.stack([out_real, out_imag], axis=2).astype(jnp.bfloat16)


def window_terms(current, band_rows, lag_rows):
    left_real = current[None, :, 0, :].astype(jnp.float32)
    left_imag = current[None, :, 1, :].astype(jnp.float32)
    right_real = band_rows[:, :, 0, :].astype(jnp.float32)
    right_imag = band_rows[:, :, 1, :].astype(jnp.float32)
    prod_real = left_real * right_real + left_imag * right_imag
    prod_imag = left_imag * right_real - left_real * right_imag
    cross_spec = jnp.stack([prod_real, prod_imag], axis=2).astype(jnp.bfloat16)
    flattened = cross_spec.reshape(band_rows.shape[0] * band_rows.shape[1], 2 * band_rows.shape[3])
    lagged = jnp.dot(flattened, lag_rows, preferred_element_type=jnp.float32)
    lagged = lagged.reshape(band_rows.shape[0], band_rows.shape[1], lag_rows.shape[1])
    return jnp.sum(lagged * lagged, axis=1)


def ring_shards(spectra, offsets, channel_group):
    windows = spectra.shape[0]
    local_chans = spectra.shape[1]
    freq_bins = spectra.shape[3]
    chan_count = lax.axis_size("chan")
    channels = local_chans * chan_count
    onehot = (channel_group[:, None] == jnp.arange(GROUPS, dtype=jnp.int32)[None, :]).astype(
        jnp.float32
    )
    chan_power = jnp.sum(jnp.square(spectra.astype(jnp.float32)), axis=(2, 3))
    partial_value = jnp.dot(chan_power, onehot, precision=lax.Precision.HIGHEST)
    group_total = lax.psum(partial_value, "chan")
    energy = group_total * (GROUPS / (freq_bins * channels))
    scales = jnp.dot(lax.rsqrt(energy + epsilon), onehot.T, precision=lax.Precision.HIGHEST)
    aligned = align_spectra(spectra, offsets, scales)
    earlier = []
    carried = aligned
    for distance in range(SPAN):
        carried = shifted(carried, "tm", 1)
        earlier.append(carried)
    buffer = jnp.concatenate(earlier[::-1] + [aligned], axis=0)
    lag_rows = lag_table(freq_bins, LAGS)
    band_len = SPAN * windows

    def one_window(window):
        current = lax.dynamic_index_in_dim(aligned, window, 0, keepdims=False)
        band_rows = lax.dynamic_slice_in_dim(buffer, window, band_len, 0)
        return window_terms(current, band_rows, lag_rows) * (1.0 / channels)

    return lax.psum_scatter(
        lax.map(
            one_window, jnp.arange(lax.axis_size("chan") * (windows // chan_count), dtype=jnp.int32)
        ).astype(jnp.bfloat16),
        "chan",
        scatter_dimension=0,
        tiled=True,
    ).astype(jnp.float32)


HIGHEST = lax.Precision.HIGHEST
ROWS = 16
FAR = 2
COLUMNS = 2
PARTS = 4


def phase_of(turns, freq_bins):
    period = 2.0 * freq_bins
    return (jnp.pi / freq_bins) * (turns - period * jnp.floor(turns / period))


def kernel(
    n, chans, windows, freq_bins, cores,
    x_ref, off_hbm, group_hbm, out_ref,
    off_ref, group_ref, local, wide, sums, tile, tile_in, al, right, left, table, acc, total, sum_out, sum_in,
    small_sem, local_sem, own_sem, e_send, e_recv, x_send, x_recv, s_send, s_recv, ready,
):
    me = lax.axis_index("tm")
    core = lax.axis_index("chan")
    levels = n // COLUMNS
    level, column = me // COLUMNS, lax.rem(me, COLUMNS)
    half = level // 2
    inner = jnp.logical_or(level == 1, level == levels - 2)
    blocks = n // 2
    mine = windows // cores
    lanes = freq_bins
    bf16 = jnp.bfloat16
    share = chans // PARTS
    tiles = share // ROWS
    mesh_id = pl.DeviceIdType.MESH

    loads = [pltpu.make_async_copy(x_ref.at[w], local.at[w], local_sem.at[w]) for w in range(windows)]
    for load in loads:
        load.start()

    barrier = pltpu.get_barrier_semaphore()
    beside = COLUMNS * level + 1 - column
    above, below = level + 1 < levels, level > 0

    def greet(sem):
        pl.semaphore_signal(sem, inc=1, device_id={"tm": beside}, device_id_type=mesh_id)

        @pl.when(above)
        def _():
            pl.semaphore_signal(sem, inc=1, device_id={"tm": me + COLUMNS}, device_id_type=mesh_id)

        @pl.when(below)
        def _():
            pl.semaphore_signal(sem, inc=1, device_id={"tm": me - COLUMNS}, device_id_type=mesh_id)

    small = [
        pltpu.make_async_copy(group_hbm, group_ref, small_sem.at[0]),
        pltpu.make_async_copy(off_hbm, off_ref, small_sem.at[1]),
    ]
    for copy in small:
        copy.start()
    near = 1 + jnp.where(above, 1, 0) + jnp.where(below, 1, 0)
    pl.semaphore_signal(barrier, inc=1, device_id={"chan": 1 - core}, device_id_type=mesh_id)
    greet(barrier)

    small[0].wait()
    frequency = lax.broadcasted_iota(jnp.int32, (freq_bins, LAGS), 0)
    shift = lax.broadcasted_iota(jnp.int32, (freq_bins, LAGS), 1) - LAGS // 2
    group_id = lax.broadcasted_iota(jnp.int32, (GROUPS, chans), 0)
    onehot = (group_id == group_ref[...]).astype(jnp.float32)
    few = onehot.astype(bf16)
    both = jnp.concatenate([few, few], axis=1)
    member = jnp.concatenate([few, few, few, few], axis=0)
    lane = lax.broadcasted_iota(jnp.int32, (windows, lanes), 1)
    row = lax.broadcasted_iota(jnp.int32, (windows, lanes), 0)

    for w in range(windows):
        loads[w].wait()
        if w == windows - 1:
            pl.semaphore_wait(barrier, near + 1)
            greet(ready.at[0])
        wide[pl.ds(w * 2 * chans, 2 * chans), :] = local[w].astype(jnp.float32)
        real = wide[pl.ds(w * 2 * chans, chans, stride=2), :]
        imag = wide[pl.ds(w * 2 * chans + 1, chans, stride=2), :]
        power = real * real + imag * imag
        high = power.astype(bf16)
        low = (power - high.astype(jnp.float32)).astype(bf16)
        sums[pl.ds(w * GROUPS, GROUPS), :] = jnp.dot(
            both, jnp.concatenate([high, low], axis=0), preferred_element_type=jnp.float32
        )
    totals = jnp.broadcast_to(jnp.sum(sums[...], axis=1, keepdims=True), sums.shape)
    tile[...] = totals
    e_copy = pltpu.make_async_remote_copy(
        src_ref=tile, dst_ref=tile_in, send_sem=e_send, recv_sem=e_recv,
        device_id={"chan": 1 - core}, device_id_type=mesh_id,
    )
    e_copy.start()

    angle = phase_of((frequency * shift).astype(jnp.float32), freq_bins)
    normaliser = 1.0 / math.sqrt(freq_bins)
    table[pl.ds(0, freq_bins), :] = (jnp.cos(angle) * normaliser).astype(bf16)
    table[pl.ds(freq_bins, freq_bins), :] = (-jnp.sin(angle) * normaliser).astype(bf16)
    small[1].wait()
    starts = jnp.zeros((windows, lanes), jnp.float32)
    for w in range(windows):
        starts = jnp.where(row == w, off_ref[w].astype(jnp.float32), starts)
    theta = phase_of(lane.astype(jnp.float32) * starts, freq_bins)
    cosine = jnp.cos(theta)
    sine = jnp.sin(theta)
    acc[...] = jnp.zeros_like(acc)
    total[:, pl.ds(0, SPAN * windows), :] = jnp.zeros((mine, SPAN * windows, LAGS), jnp.float32)

    pl.semaphore_wait(ready.at[0], near)
    greet(ready.at[1])
    e_copy.wait_recv()
    energy = (totals + tile_in[...]) * (GROUPS / (freq_bins * chans * cores))
    scales = lax.rsqrt(energy + epsilon)

    for w in range(windows):
        factor = scales[w * GROUPS : (w + 1) * GROUPS]
        turn = jnp.concatenate([factor * cosine[w : w + 1], factor * sine[w : w + 1]], axis=1)
        top = turn.astype(bf16)
        rest = turn - top.astype(jnp.float32)
        middle = rest.astype(bf16)
        bottom = (rest - middle.astype(jnp.float32)).astype(bf16)
        pieces = jnp.concatenate([top, middle, bottom, jnp.zeros_like(top)], axis=0)
        factors = lax.dot_general(
            member, pieces, (((0,), (0,)), ((), ())), preferred_element_type=jnp.float32
        )
        real = wide[pl.ds(w * 2 * chans, chans, stride=2), :]
        imag = wide[pl.ds(w * 2 * chans + 1, chans, stride=2), :]
        turn_cos, turn_sin = factors[:, :lanes], factors[:, lanes:]
        out = (real * turn_cos + imag * turn_sin, imag * turn_cos - real * turn_sin)
        for r in range(2):
            al[:, w, :, r] = out[r].astype(bf16).reshape(PARTS, tiles, ROWS, freq_bins)

    def routes():
        def inside(own, flip):
            place = COLUMNS * (half if own else 1 - half) + lax.rem(column + core + flip, 2)
            return COLUMNS + place, place, 0, 2 * (1 - own) + flip

        yield inside(1, 0)
        yield inside(1, 1)
        yield inside(0, 0)
        yield inside(0, 1)
        for part in range(2):
            for flip in range(COLUMNS):
                place = lax.rem(column + core + flip, 2)
                yield (n - COLUMNS) * half + place, 2 * place + part, part, 4 + 2 * part + flip

    def x_copy(there, first, part, index, source):
        return pltpu.make_async_remote_copy(
            src_ref=al.at[first],
            dst_ref=right.at[source, part],
            send_sem=x_send.at[index],
            recv_sem=x_recv.at[source, part],
            device_id={"tm": there},
            device_id_type=mesh_id,
        )

    def own_copy(first, part):
        return pltpu.make_async_copy(al.at[first], right.at[me, part], own_sem.at[part])

    ways = list(routes())

    def send(index):
        there, first, part, index = ways[index]

        @pl.when(there == me)
        def _():
            own_copy(first, part).start()

        @pl.when(there != me)
        def _():
            x_copy(there, first, part, index, me).start()

    @pl.when(inner)
    def _():
        for index in (0, 1, 4, 5, 6, 7, 2, 3):
            send(index)

    @pl.when(jnp.logical_not(inner))
    def _():
        for index in (0, 1, 4, 5, 6, 7, 2, 3):
            if index == FAR:
                pl.semaphore_wait(ready.at[1], near)
            send(index)

    @pl.when(inner)
    def _():
        pl.semaphore_wait(ready.at[1], near)

    greet(ready.at[2])

    bit = lax.rem(level, 2)

    def block(base, flip, k):
        turned = core * jnp.maximum(flip, k // 2)
        return base + COLUMNS * lax.rem(bit + flip + k // 2, 2) + lax.rem(column + turned + lax.rem(k, 2), 2)

    here, away = blocks * half, blocks * (1 - half)

    def job(sets, part):
        for w in range(windows):
            rows = []
            for upper, lower in sets:
                for i in range(tiles):
                    left_real = left[upper, part, w, i, 0].astype(bf16)
                    left_imag = left[upper, part, w, i, 1].astype(bf16)
                    for v in range(windows):
                        right_real = right[lower, part, v, i, 0]
                        right_imag = right[lower, part, v, i, 1]
                        rows.append(
                            jnp.concatenate(
                                [
                                    left_real * right_real + left_imag * right_imag,
                                    left_imag * right_real - left_real * right_imag,
                                ],
                                axis=1,
                            )
                        )
            lagged = jnp.dot(jnp.concatenate(rows, axis=0), table[...], preferred_element_type=jnp.float32)
            lagged = lagged.reshape(len(sets), tiles, windows, ROWS // 8, 8, LAGS)
            squares = jnp.sum(lagged * lagged, axis=(1, 3))
            for k, (upper, lower) in enumerate(sets):
                up, low = lax.rem(upper, blocks), lax.rem(lower, blocks)
                acc[up, w, pl.ds(low * windows * 8, windows * 8), :] += squares[k].reshape(windows * 8, LAGS)

    holder = cores * jnp.where(inner, me - COLUMNS, 2 * COLUMNS + column) + core
    crossing, holders = 2 * COLUMNS * cores, 3 * COLUMNS * cores

    def s_copy(up, low, k, there, source):
        return pltpu.make_async_remote_copy(
            src_ref=sum_out.at[up, low, k],
            dst_ref=sum_in.at[source, low],
            send_sem=s_send.at[up, low, k],
            recv_sem=s_recv.at[source, low],
            device_id={"tm": there, "chan": k},
            device_id_type=mesh_id,
        )

    def hand_over(upper, lower):
        up, low = lax.rem(upper, blocks), lax.rem(lower, blocks)
        for k in range(cores):
            result = []
            for j in range(mine):
                held = [
                    acc[up, k * mine + j, pl.ds(low * windows * 8 + i, windows, stride=8), :] for i in range(8)
                ]
                while len(held) > 1:
                    held = [one + two for one, two in zip(held[::2], held[1::2])]
                result.append(held[0])
            sum_out[up, low, k] = jnp.stack(result, axis=0).astype(bf16)

            @pl.when(jnp.logical_or(upper != me, core != k))
            def _():
                s_copy(up, low, k, upper, holder).start()

            @pl.when(jnp.logical_and(upper == me, core == k))
            def _():
                sum_in[holder, low] = sum_out[up, low, k]

    def place_of(q):
        part = jnp.where(inner, 0, q // blocks)
        i = lax.rem(q, blocks)
        far = jnp.logical_and(inner, q >= blocks)
        t = jnp.where(far, block(away, 1, 2 * lax.rem(i, 2) + i // 2), block(here, 0, i))
        count = jnp.where(inner, jnp.where(far, blocks, 0), i + 1)
        done = jnp.where(jnp.logical_or(inner, part == 1), count, 0)
        return t, part, count, done

    def ordered(t, k):
        other = block(here, 0, k)
        return jnp.maximum(t, other), jnp.minimum(t, other)

    def step(q, carry):
        t, part, count, done = place_of(q)

        @pl.when(t == me)
        def _():
            own_copy(0, part).wait()

        @pl.when(t != me)
        def _():
            x_copy(me, 0, part, 0, t).wait_recv()

        left[t, part] = right[t, part].astype(jnp.float32)

        @pl.when(q == 1)
        def _():
            pl.semaphore_wait(ready.at[2], near)

        finished = done > 0

        def two_jobs(k, inside):
            sets = [ordered(t, 2 * k), ordered(t, 2 * k + 1)]
            job(sets, part)

            @pl.when(finished)
            def _():
                for upper, lower in sets:
                    hand_over(upper, lower)

            return inside

        lax.fori_loop(0, count // 2, two_jobs, 0)

        @pl.when(lax.rem(count, 2) == 1)
        def _():
            upper, lower = ordered(t, count - 1)
            job([(upper, lower)], part)

            @pl.when(finished)
            def _():
                hand_over(upper, lower)

        return carry

    lax.fori_loop(0, n, step, 0)

    def collect(first, last, low):
        result = None
        for source in range(first, last):
            @pl.when(jnp.logical_or(source != holder, jnp.logical_not(keeps)))
            def _():
                s_copy(0, low, 0, me, source).wait_recv()

            value = sum_in[source, low].astype(jnp.float32)
            result = value if result is None else result + value
        return result

    target = blocks * jnp.where(inner, 1, half)
    keeps = jnp.logical_and(me >= target, me < target + blocks)
    base = SPAN * windows
    for low in range(blocks):
        @pl.when(low <= lax.rem(me, blocks))
        def _():
            total[:, pl.ds(base + (blocks * half + low) * windows, windows), :] = collect(crossing, holders, low)

    for low in range(blocks):
        @pl.when(half == 1)
        def _():
            total[:, pl.ds(base + low * windows, windows), :] = collect(crossing // 2, crossing, low)

    for low in range(blocks):
        @pl.when(half == 1)
        def _():
            total[:, pl.ds(base + low * windows, windows), :] += collect(0, crossing // 2, low)

    for j in range(mine):
        out_ref[j] = total[j, pl.ds(me * windows + core * mine + j, base), :] * (1.0 / (chans * cores))

    for there, first, part, index in ways:
        @pl.when(there != me)
        def _():
            x_copy(there, first, part, index, me).wait_send()

    def sent(q, carry):
        t, _, _, done = place_of(q)

        def one_block(k, inside):
            upper, lower = ordered(t, k)
            for c in range(cores):
                @pl.when(jnp.logical_or(upper != me, core != c))
                def _():
                    s_copy(lax.rem(upper, blocks), lax.rem(lower, blocks), c, upper, holder).wait_send()

            return inside

        lax.fori_loop(0, done, one_block, 0)
        return carry

    lax.fori_loop(0, n, sent, 0)
    e_copy.wait_send()


def spread_shards(spectra, offsets, channel_group):
    windows, chans, _, freq_bins = spectra.shape
    n = lax.axis_size("tm")
    cores = lax.axis_size("chan")
    blocks = n // 2
    band = SPAN * windows
    mine = windows // cores
    dma = pltpu.SemaphoreType.DMA
    pieces = (windows, chans // PARTS // ROWS, 2, ROWS, freq_bins)
    return pl.pallas_call(
        functools.partial(kernel, n, chans, windows, freq_bins, cores),
        out_shape=pltpu.VMEM((mine, band, LAGS), jnp.float32),
        in_specs=[
            pl.BlockSpec(memory_space=pl.ANY),
            pl.BlockSpec(memory_space=pl.ANY),
            pl.BlockSpec(memory_space=pl.ANY),
        ],
        out_specs=pl.BlockSpec(memory_space=pltpu.VMEM),
        scratch_shapes=[
            pltpu.SMEM((windows,), jnp.int32),
            pltpu.VMEM((1, chans), jnp.int32),
            pltpu.VMEM((windows, 2 * chans, freq_bins), jnp.bfloat16),
            pltpu.VMEM((windows * 2 * chans, freq_bins), jnp.float32),
            pltpu.VMEM((windows * GROUPS, freq_bins), jnp.float32),
            pltpu.VMEM((windows * GROUPS, freq_bins), jnp.float32),
            pltpu.VMEM((windows * GROUPS, freq_bins), jnp.float32),
            pltpu.VMEM((PARTS,) + pieces, jnp.bfloat16),
            pltpu.VMEM((n, 2) + pieces, jnp.bfloat16),
            pltpu.VMEM((n, 2) + pieces, jnp.float32),
            pltpu.VMEM((2 * freq_bins, LAGS), jnp.bfloat16),
            pltpu.VMEM((blocks, windows, blocks * windows * 8, LAGS), jnp.float32),
            pltpu.VMEM((mine, band + n * windows, LAGS), jnp.float32),
            pltpu.VMEM((blocks, blocks, cores, mine, windows, LAGS), jnp.bfloat16),
            pltpu.VMEM((3 * COLUMNS * cores, blocks, mine, windows, LAGS), jnp.bfloat16),
            dma((2,)), dma((windows,)), dma((2,)), dma, dma, dma((n,)), dma((n, 2)),
            dma((blocks, blocks, cores)), dma((3 * COLUMNS * cores, blocks)), pltpu.SemaphoreType.REGULAR((3,)),
        ],
        compiler_params=pltpu.CompilerParams(
            collective_id=0, has_side_effects=True, vmem_limit_bytes=56 * 1024 * 1024
        ),
    )(spectra.reshape(windows, 2 * chans, freq_bins), offsets, channel_group.reshape(1, chans))


def shards(spectra, offsets, channel_group):
    windows, chans, _, freq_bins = spectra.shape
    n = lax.axis_size("tm")
    fits = (
        chans == freq_bins == LAGS == 128
        and windows == 8
        and lax.axis_size("chan") == 2
        and n == 8
    )
    return (spread_shards if fits else ring_shards)(spectra, offsets, channel_group)


def solution(mesh):
    placed = (P(("arrays", "tm"), "chan", None, None), P(("arrays", "tm")), P(("arrays", "chan")))
    return jax.shard_map(
        shards,
        mesh=mesh,
        in_specs=placed,
        out_specs=P(("arrays", "tm", "chan"), None, None),
        check_vma=False,
    )
```
